256 devices in a mesh: blk: 4 (over y_hi, core), dp: 64 (over z, x, y_lo).
Axes of the slice: x: 4, y: 4 (y_hi: 2, y_lo: 2; y = y_hi * 2 + y_lo), z: 8, core: 2. Of those that a mesh axis runs over, the one named last changes fastest.
Arguments:
- fingerprints: bfloat16 [98304, 2048], P(('blk', 'dp')), may hold values from 0 to 3, as said below
- w_first: bfloat16 [2048, 1024], replicated, may hold values from -0.3125 to 0.3125
- w_second: bfloat16 [1024, 512], replicated, may hold values from -0.0625 to 0.0625
Outputs:
- grad_first: float32 [2048, 1024], P('dp')
- grad_second: float32 [1024, 512], P('dp')
The draws below stay inside these ranges and needn't reach their ends.
Inputs may be any that keep to these rules, and one draw needn't show every extreme that they name: `fingerprints`: Non-negative feature weights; every molecule has a third or more of its features nonzero.
All inputs are finite; a program needn't handle non-finite values.
Results may differ from the reference program's by a relative error of at most 0.003.
Values may be sent and summed in bfloat16 or wider, within the bound.
A program may use at most 64 MiB of HBM per device.

```python
import math
import jax
import jax.numpy as jnp
from jax import lax

D_IN = 2048
HID = 1024
EMB = 512
TOK_DEV = 384
GROUP = 1536
MOLS = 98304
N_BLK = 4
N_DP = 64


def draw_fingerprints(key, part):
    keys = jax.random.split(jax.random.fold_in(key, 11), 9)
    scaffolds = max(GROUP // 24, 4)
    member = jax.random.randint(keys[0], (MOLS,), 0, scaffolds).astype(jnp.int32)
    scaffold_present = jax.random.uniform(keys[1], (scaffolds, D_IN), jnp.float32) < 0.45
    scaffold_mag = jnp.exp(jax.random.uniform(keys[2], (scaffolds, D_IN), jnp.float32, math.log(0.05), 0.0))
    own_mag = jnp.exp(jax.random.uniform(keys[8], (MOLS, D_IN), jnp.float32, math.log(0.05), 0.0))
    column = jnp.exp(jax.random.uniform(keys[3], (1, D_IN), jnp.float32, -1.0, 1.0))
    keep = jax.random.uniform(keys[4], (MOLS, D_IN), jnp.float32) < 0.85
    own_density = jax.random.uniform(keys[5], (MOLS, 1), jnp.float32, 0.1, 0.3)
    own_present = jax.random.uniform(keys[6], (MOLS, D_IN), jnp.float32) < own_density
    jitter = jax.random.uniform(keys[7], (MOLS, D_IN), jnp.float32, 0.8, 1.1)
    shared_present = jnp.take(scaffold_present, member, axis=0) & keep
    shared_mag = jnp.take(scaffold_mag, member, axis=0) * jitter
    values = jnp.where(shared_present, shared_mag, jnp.where(own_present, own_mag, 0.0))
    values = values * column
    return values.astype(jnp.bfloat16)


def centred(stream_key, extent, spread, limit, dtype=jnp.bfloat16):
    result = jax.random.normal(stream_key, extent, jnp.float32) * spread
    return jnp.minimum(jnp.maximum(result, -limit), limit).astype(dtype)


def setup_inputs(seed: int = 0) -> dict:
    streams_of = jax.random.split(jax.random.key(seed), 4)
    fingerprints = draw_fingerprints(jax.random.fold_in(streams_of[3], 71), 0)
    w_first = centred(streams_of[1], (D_IN, HID), 0.05, 0.3125)
    w_second = centred(streams_of[2], (HID, EMB), 0.01, 0.0625)
    return {"fingerprints": fingerprints, "w_first": w_first, "w_second": w_second}


def group_terms(pair):
    feats, embeds = pair
    sqn = lax.optimization_barrier(jnp.sum(jnp.square(feats.astype(jnp.float32)), axis=1))
    inter = jnp.dot(feats, feats.T, preferred_element_type=jnp.float32)
    tanimoto = inter / (sqn[:, None] + sqn[None, :] - inter)
    pred = jnp.dot(embeds, embeds.T, preferred_element_type=jnp.float32) * (1.0 / math.sqrt(EMB))
    resid = (pred - tanimoto).astype(jnp.bfloat16)
    return jnp.dot(resid, embeds, preferred_element_type=jnp.float32)

def reference(fingerprints, w_first, w_second):
    pre = jnp.dot(fingerprints, w_first, preferred_element_type=jnp.float32)
    sig = jax.nn.sigmoid(pre)
    hidden = (pre * sig).astype(jnp.bfloat16)
    embed = jnp.dot(hidden, w_second, preferred_element_type=jnp.float32).astype(jnp.bfloat16)
    feats = fingerprints.reshape(N_BLK, N_DP, TOK_DEV, D_IN).transpose(1, 0, 2, 3).reshape(N_DP, GROUP, D_IN)
    embeds = embed.reshape(N_BLK, N_DP, TOK_DEV, EMB).transpose(1, 0, 2, 3).reshape(N_DP, GROUP, EMB)
    summed = lax.map(group_terms, (feats, embeds))
    summed = summed.reshape(N_DP, N_BLK, TOK_DEV, EMB).transpose(1, 0, 2, 3).reshape(MOLS, EMB)
    dembed = (summed * (2.0 / math.sqrt(GROUP * MOLS))).astype(jnp.bfloat16)
    dhidden = jnp.dot(dembed, w_second.T, preferred_element_type=jnp.float32)
    dpre = (dhidden * sig * (1.0 + pre * (1.0 - sig))).astype(jnp.bfloat16)
    grad_second = jnp.dot(hidden.T, dembed, preferred_element_type=jnp.float32)
    grad_first = jnp.dot(fingerprints.T, dpre, preferred_element_type=jnp.float32)
    return (grad_first, grad_second)
```

```python
import functools
import math

import jax
import jax.numpy as jnp
from jax import lax
from jax.experimental import pallas as pl
from jax.experimental.pallas import tpu as pltpu
from jax.sharding import PartitionSpec as P

MESH = pl.DeviceIdType.MESH
F32 = jnp.float32
BF16 = jnp.bfloat16
NZ, NX = 8, 4
T = 256
HALF = 128


def dot_nt(a, b):
    return lax.dot_general(a, b, (((1,), (1,)), ((), ())), preferred_element_type=F32)


def dot_nn(a, b):
    return jnp.dot(a, b, preferred_element_type=F32)


def group_kernel(
    scale, fp_in, w1_in, w2_in, g1_out, g2_out,
    fp, fpt, w1, w2, hid, hidt, emb, summed, gate, demb, dpre, sqc, sqr,
    load_sem, send_sem, recv_sem, pass_send, pass_recv,
):
    blk = lax.axis_index("blk")
    tok, d_in = fp_in.shape
    width = w1_in.shape[1]
    half = 2 * tok
    pieces = tok // HALF
    groups = (4 * tok) // T
    local = half // T
    far = {"blk": (blk + 2) % 4}
    near = {"blk": (blk // 2) * 2 + 1 - blk % 2}

    barrier = pltpu.get_barrier_semaphore()
    for peer in (far, near):
        pl.semaphore_signal(barrier, inc=1, device_id=peer, device_id_type=MESH)
    loads = [
        pltpu.make_async_copy(fp_in, fp.at[pl.ds(0, tok)], load_sem.at[0]),
        pltpu.make_async_copy(w1_in, w1, load_sem.at[1]),
        pltpu.make_async_copy(w2_in, w2, load_sem.at[2]),
    ]
    for load in loads:
        load.start()
    pl.semaphore_wait(barrier, 2)

    def remote(src, dst, send, recv, peer):
        return pltpu.make_async_remote_copy(
            src_ref=src, dst_ref=dst, send_sem=send, recv_sem=recv,
            device_id=peer, device_id_type=MESH,
        )

    far_copies = [
        remote(
            fp_in.at[pl.ds(p * HALF, HALF)], fp.at[pl.ds(half + p * T, HALF)],
            send_sem.at[p], recv_sem.at[p], far,
        )
        for p in range(pieces)
    ]
    near_copy = remote(
        fp_in, fp.at[pl.ds(tok, tok)], send_sem.at[pieces], recv_sem.at[pieces], near
    )
    for copy in far_copies:
        copy.start()
    near_copy.start()

    def passing(p):
        return remote(
            fp.at[pl.ds(half + p * T, HALF)], fp.at[pl.ds(half + p * T + HALF, HALF)],
            pass_send.at[p], pass_recv.at[p], near,
        )

    summed[...] = jnp.zeros_like(summed)
    for load in loads:
        load.wait()

    def encode(p):
        rows = pl.ds(p * T, T)

        @pl.loop(0, width // T)
        def _(n):
            cols = pl.ds(pl.multiple_of(n * T, T), T)
            pre = dot_nn(fp[rows, :], w1[:, cols])
            sig = 1.0 / (1.0 + jnp.exp(-pre))
            h = (pre * sig).astype(BF16)
            hid[:, cols] = h
            hidt[cols, rows] = h.T

            @pl.when(n == blk)
            def _():
                gate[rows, :] = sig * (1.0 + pre * (1.0 - sig))

        emb[rows, :] = dot_nn(hid[...], w2[...]).astype(BF16)

        @pl.loop(0, d_in // T)
        def _(n):
            cols = pl.ds(pl.multiple_of(n * T, T), T)
            fpt[cols, rows] = fp[rows, cols].T

    def residual(i, p, inter):
        den = sqc[pl.ds(i * T, T), :][:, :1] + sqr[:1, pl.ds(p * T, T)] - inter
        pred = dot_nt(emb[pl.ds(i * T, T), :], emb[pl.ds(p * T, T), :])
        return (pred * (1.0 / math.sqrt(emb.shape[1])) - inter / den).astype(BF16)

    def pairs(p):
        rows = pl.ds(p * T, T)
        inter = dot_nt(fp[rows, :], fp[rows, :])
        r_id = lax.broadcasted_iota(jnp.int32, (T, T), 0)
        c_id = lax.broadcasted_iota(jnp.int32, (T, T), 1)
        diag = jnp.where(r_id == c_id, inter, 0.0)
        sqc[rows, :] = jnp.broadcast_to(jnp.sum(diag, axis=1, keepdims=True), (T, 128))
        sqr[:, rows] = jnp.broadcast_to(jnp.sum(diag, axis=0, keepdims=True), (8, T))
        resid = residual(p, p, inter)
        summed[rows, :] += dot_nn(resid, emb[rows, :])

        def other(i, carry):
            above = pl.ds(pl.multiple_of(i * T, T), T)
            resid = residual(i, p, dot_nt(fp[above, :], fp[rows, :]))
            summed[above, :] += dot_nn(resid, emb[rows, :])
            summed[rows, :] += dot_nn(resid.T, emb[above, :])
            return carry

        lax.fori_loop(0, p, other, 0)

    @pl.loop(0, groups)
    def _(p):
        p = jnp.int32(p)

        @pl.when(p == 1)
        def _():
            near_copy.wait()

        for k in range(pieces):

            @pl.when(p == local + k)
            def _(k=k):
                far_copies[k].wait()
                passing(k).start()
                passing(k).wait()

        encode(pl.multiple_of(p, 1))
        pairs(pl.multiple_of(p, 1))

    demb[...] = (summed[...] * scale).astype(BF16)

    @pl.loop(0, groups)
    def _(i):
        rows = pl.ds(pl.multiple_of(i * T, T), T)
        back = dot_nt(demb[rows, :], w2[pl.ds(pl.multiple_of(blk * T, T), T), :])
        dpre[rows, :] = (back * gate[rows, :]).astype(BF16)

    @pl.loop(0, NZ)
    def _(z):
        step = d_in // NZ
        part = dot_nn(fpt[pl.ds(pl.multiple_of(z * step, step), step), :], dpre[...])
        sub = step // NX
        for x in range(NX):
            g1_out[x, pl.ds(pl.multiple_of(z * sub, sub), sub), :] = part[
                x * sub : (x + 1) * sub
            ].astype(BF16)
        cols = demb.shape[1] // 4
        step = width // NZ
        part = dot_nn(
            hidt[pl.ds(pl.multiple_of(z * step, step), step), :],
            demb[:, pl.ds(pl.multiple_of(blk * cols, cols), cols)],
        )
        sub = step // NX
        for x in range(NX):
            g2_out[x, pl.ds(pl.multiple_of(z * sub, sub), sub), :] = part[
                x * sub : (x + 1) * sub
            ].astype(BF16)


def group_gradients(fingerprints, w_first, w_second, scale):
    tok, d_in = fingerprints.shape
    hidden, width = w_second.shape
    rows = 4 * tok
    pieces = tok // HALF
    any_spec = pl.BlockSpec(memory_space=pl.ANY)
    vmem_spec = pl.BlockSpec(memory_space=pltpu.VMEM)
    return pl.pallas_call(
        functools.partial(group_kernel, scale),
        out_shape=(
            jax.ShapeDtypeStruct((NX, d_in // NX, hidden // 4), BF16),
            jax.ShapeDtypeStruct((NX, hidden // NX, width // 4), BF16),
        ),
        in_specs=[any_spec] * 3,
        out_specs=(vmem_spec, vmem_spec),
        scratch_shapes=[
            pltpu.VMEM((rows, d_in), BF16),
            pltpu.VMEM((d_in, rows), BF16),
            pltpu.VMEM((d_in, hidden), BF16),
            pltpu.VMEM((hidden, width), BF16),
            pltpu.VMEM((T, hidden), BF16),
            pltpu.VMEM((hidden, rows), BF16),
            pltpu.VMEM((rows, width), BF16),
            pltpu.VMEM((rows, width), F32),
            pltpu.VMEM((rows, hidden // 4), F32),
            pltpu.VMEM((rows, width), BF16),
            pltpu.VMEM((rows, hidden // 4), BF16),
            pltpu.VMEM((rows, 128), F32),
            pltpu.VMEM((8, rows), F32),
            pltpu.SemaphoreType.DMA((3,)),
            pltpu.SemaphoreType.DMA((pieces + 1,)),
            pltpu.SemaphoreType.DMA((pieces + 1,)),
            pltpu.SemaphoreType.DMA((pieces,)),
            pltpu.SemaphoreType.DMA((pieces,)),
        ],
        compiler_params=pltpu.CompilerParams(
            collective_id=0, has_side_effects=True, vmem_limit_bytes=56 << 20
        ),
        name="group_gradients",
    )(fingerprints, w_first, w_second)


def reduce_kernel(
    g1, g2, o1, o2, own1, own2, xb1, xb2, zs1, zs2, zb1, zb2, ys1, ys2, yb1, yb2,
    load_sem, xs, xr, zs, zr, ys, yr,
):
    blk = lax.axis_index("blk")
    dp = lax.axis_index("dp")
    z, x = dp // 8, (dp // 2) % 4
    y, c = (blk // 2) * 2 + dp % 2, blk % 2

    def at(z, x, y, c):
        return {"blk": (y // 2) * 2 + c, "dp": (z * NX + x) * 2 + y % 2}

    x_peers = [at(z, (x + k) % NX, y, c) for k in range(1, NX)]
    z_peers = [at((z + k) % NZ, x, y, c) for k in range(1, NZ)]
    y_steps = [(dy, dc) for dy in range(4) for dc in range(2)][1:]
    y_peers = [at(z, x, (y + dy) % 4, (c + dc) % 2) for dy, dc in y_steps]
    barrier = pltpu.get_barrier_semaphore()
    for peer in x_peers + z_peers + y_peers:
        pl.semaphore_signal(barrier, inc=1, device_id=peer, device_id_type=MESH)
    loads = [
        pltpu.make_async_copy(g1.at[x], own1, load_sem.at[0]),
        pltpu.make_async_copy(g2.at[x], own2, load_sem.at[1]),
    ]
    for load in loads:
        load.start()
    pl.semaphore_wait(barrier, len(x_peers) + len(z_peers) + len(y_peers))

    def remote(src, dst, send, recv, peer):
        return pltpu.make_async_remote_copy(
            src_ref=src, dst_ref=dst, send_sem=send, recv_sem=recv,
            device_id=peer, device_id_type=MESH,
        )

    copies = []
    for k in (2, 1, 3):
        peer, to = x_peers[k - 1], (x + k) % NX
        copies.append(remote(g1.at[to], xb1.at[k - 1], xs.at[0, k - 1], xr.at[0, k - 1], peer))
        copies.append(remote(g2.at[to], xb2.at[k - 1], xs.at[1, k - 1], xr.at[1, k - 1], peer))
    for copy in copies:
        copy.start()
    for load in loads:
        load.wait()
    for copy in copies:
        copy.wait()

    def sum_x(own, buf):
        total = own[...].astype(F32)
        for k in range(NX - 1):
            total = total + buf[k].astype(F32)
        return total

    zs1[...] = sum_x(own1, xb1).astype(BF16).reshape(zs1.shape)
    zs2[...] = sum_x(own2, xb2).astype(BF16).reshape(zs2.shape)

    copies = []
    for k in (4, 3, 5, 2, 6, 1, 7):
        peer, to = z_peers[k - 1], (z + k) % NZ
        copies.append(remote(zs1.at[to], zb1.at[k - 1], zs.at[0, k - 1], zr.at[0, k - 1], peer))
        copies.append(remote(zs2.at[to], zb2.at[k - 1], zs.at[1, k - 1], zr.at[1, k - 1], peer))
    for copy in copies:
        copy.start()
    for copy in copies:
        copy.wait()

    def sum_z(own, buf):
        total = own[z].astype(F32)
        for k in range(NZ - 1):
            total = total + buf[k].astype(F32)
        return total

    ys1[...] = sum_z(zs1, zb1).reshape(ys1.shape)
    ys2[...] = sum_z(zs2, zb2).reshape(ys2.shape)

    copies = []
    for k, (dy, dc) in enumerate(y_steps):
        peer, to = y_peers[k], (y + dy) % 2
        slot = y * 2 + c
        copies.append(remote(ys1.at[to], yb1.at[slot], ys.at[0, k], yr.at[0, k], peer))
        copies.append(remote(ys2.at[to], yb2.at[slot], ys.at[1, k], yr.at[1, k], peer))
    for copy in copies:
        copy.start()
    yb1[y * 2 + c] = ys1[y % 2]
    yb2[y * 2 + c] = ys2[y % 2]
    for copy in copies:
        copy.wait()
    for h in range(2):
        for core in range(2):
            quarter = 2 * h + core
            low, high = 4 * h + core, 4 * h + 2 + core
            o1[:, quarter * o1.shape[1] // 4 : (quarter + 1) * o1.shape[1] // 4] = (
                yb1[low] + yb1[high]
            )
            o2[:, quarter * o2.shape[1] // 4 : (quarter + 1) * o2.shape[1] // 4] = (
                yb2[low] + yb2[high]
            )


def reduce_gradients(g1, g2):
    vmem_spec = pl.BlockSpec(memory_space=pltpu.VMEM)
    any_spec = pl.BlockSpec(memory_space=pl.ANY)
    _, r1, c1 = g1.shape
    _, r2, c2 = g2.shape
    z1, z2 = r1 // NZ, r2 // NZ
    return pl.pallas_call(
        reduce_kernel,
        out_shape=(
            jax.ShapeDtypeStruct((z1 // 2, 4 * c1), F32),
            jax.ShapeDtypeStruct((z2 // 2, 4 * c2), F32),
        ),
        in_specs=[any_spec] * 2,
        out_specs=(vmem_spec, vmem_spec),
        scratch_shapes=[
            pltpu.VMEM((r1, c1), BF16),
            pltpu.VMEM((r2, c2), BF16),
            pltpu.VMEM((NX - 1, r1, c1), BF16),
            pltpu.VMEM((NX - 1, r2, c2), BF16),
            pltpu.VMEM((NZ, z1, c1), BF16),
            pltpu.VMEM((NZ, z2, c2), BF16),
            pltpu.VMEM((NZ - 1, z1, c1), BF16),
            pltpu.VMEM((NZ - 1, z2, c2), BF16),
            pltpu.VMEM((2, z1 // 2, c1), F32),
            pltpu.VMEM((2, z2 // 2, c2), F32),
            pltpu.VMEM((8, z1 // 2, c1), F32),
            pltpu.VMEM((8, z2 // 2, c2), F32),
            pltpu.SemaphoreType.DMA((2,)),
            pltpu.SemaphoreType.DMA((2, NX - 1)),
            pltpu.SemaphoreType.DMA((2, NX - 1)),
            pltpu.SemaphoreType.DMA((2, NZ - 1)),
            pltpu.SemaphoreType.DMA((2, NZ - 1)),
            pltpu.SemaphoreType.DMA((2, 7)),
            pltpu.SemaphoreType.DMA((2, 7)),
        ],
        compiler_params=pltpu.CompilerParams(
            collective_id=1, has_side_effects=True, vmem_limit_bytes=40 << 20
        ),
        name="reduce_gradients",
    )(g1, g2)


def per_device(fingerprints, w_first, w_second):
    group_rows = fingerprints.shape[0] * lax.axis_size("blk")
    all_rows = group_rows * lax.axis_size("dp")
    scale = 2.0 / math.sqrt(group_rows * all_rows)
    g1, g2 = group_gradients(fingerprints, w_first, w_second, scale)
    return reduce_gradients(g1, g2)


def solution(mesh):
    in_specs = (P(("blk", "dp"), None), P(), P())
    out_specs = (P("dp", None), P("dp", None))
    return jax.shard_map(
        per_device, mesh=mesh, in_specs=in_specs, out_specs=out_specs, check_vma=False
    )
```

```python
import functools
import math

import jax
import jax.numpy as jnp
from jax import lax
from jax.experimental import pallas as pl
from jax.experimental.pallas import tpu as pltpu
from jax.sharding import PartitionSpec as P

MESH = pl.DeviceIdType.MESH
F32 = jnp.float32
BF16 = jnp.bfloat16
NZ, NX = 8, 4
T = 256
HALF = 128


def dot_nt(a, b):
    return lax.dot_general(a, b, (((1,), (1,)), ((), ())), preferred_element_type=F32)


def dot_nn(a, b):
    return jnp.dot(a, b, preferred_element_type=F32)


def step_kernel(
    scale, fp_in, w1_in, w2_in, o1, o2,
    fp, fpt, w1, w2, hid, hidt, emb, summed, gate, demb, dpre, sqc, sqr,
    xo1, xo2, xb1, xb2, zs1, zs2, zb1, zb2, ys1, ys2, yb1, yb2,
    load_sem, send_sem, recv_sem, pass_send, pass_recv, xs, xr, zs, zr, ys, yr,
):
    blk = lax.axis_index("blk")
    dp = lax.axis_index("dp")
    z, x = dp // 8, (dp // 2) % 4
    y, c = (blk // 2) * 2 + dp % 2, blk % 2
    tok, d_in = fp_in.shape
    hidden, width = w2_in.shape
    half = 2 * tok
    rows_all = 4 * tok
    pieces = tok // HALF
    norm = 1.0 / math.sqrt(width)

    def at(z, x, y, c):
        return {"blk": (y // 2) * 2 + c, "dp": (z * NX + x) * 2 + y % 2}

    far = at(z, x, (y + 2) % 4, c)
    near = at(z, x, y, 1 - c)
    x_peers = [at(z, (x + k) % NX, y, c) for k in range(1, NX)]
    z_peers = [at((z + k) % NZ, x, y, c) for k in range(1, NZ)]
    y_steps = [(dy, dc) for dy in range(4) for dc in range(2)][1:]
    y_peers = [at(z, x, (y + dy) % 4, (c + dc) % 2) for dy, dc in y_steps]

    barrier = pltpu.get_barrier_semaphore()
    for peer in y_peers + x_peers + z_peers:
        pl.semaphore_signal(barrier, inc=1, device_id=peer, device_id_type=MESH)
    loads = [
        pltpu.make_async_copy(fp_in, fp.at[pl.ds(0, tok)], load_sem.at[0]),
        pltpu.make_async_copy(w1_in, w1, load_sem.at[1]),
        pltpu.make_async_copy(w2_in, w2, load_sem.at[2]),
    ]
    for load in loads:
        load.start()
    pl.semaphore_wait(barrier, len(x_peers) + len(z_peers) + len(y_peers))

    def remote(src, dst, send, recv, peer):
        return pltpu.make_async_remote_copy(
            src_ref=src, dst_ref=dst, send_sem=send, recv_sem=recv,
            device_id=peer, device_id_type=MESH,
        )

    def far_copy(p):
        return remote(
            fp_in.at[pl.ds(p * HALF, HALF)], fp.at[pl.ds(half + p * T, HALF)],
            send_sem.at[p], recv_sem.at[p], far,
        )

    def passing(p):
        return remote(
            fp.at[pl.ds(half + p * T, HALF)], fp.at[pl.ds(half + p * T + HALF, HALF)],
            pass_send.at[p], pass_recv.at[p], near,
        )

    near_copy = remote(
        fp_in, fp.at[pl.ds(tok, tok)], send_sem.at[pieces], recv_sem.at[pieces], near
    )
    for p in range(pieces):
        far_copy(p).start()
    near_copy.start()
    for load in loads:
        load.wait()
    near_copy.wait()

    def encode_columns(rows, cols):
        pre = dot_nn(fp[rows, :], w1[:, cols])
        sig = 1.0 / (1.0 + jnp.exp(-pre))
        h = (pre * sig).astype(BF16)
        hid[pl.ds(0, h.shape[0]), cols] = h
        hidt[cols, rows] = h.T
        gate[rows, cols] = sig * (1.0 + pre * (1.0 - sig))

    def embed(rows, count):
        emb[rows, :] = dot_nn(hid[pl.ds(0, count), :], w2[...]).astype(BF16)

    def residual(upper, lower):
        inter = dot_nt(fp[upper, :], fp[lower, :])
        den = sqc[upper, :][:, :1] + sqr[:1, lower] - inter
        pred = dot_nt(emb[upper, :], emb[lower, :])
        return (pred * norm - inter / den).astype(BF16)

    def diagonal(rows):
        inter = dot_nt(fp[rows, :], fp[rows, :])
        r_id = lax.broadcasted_iota(jnp.int32, (T, T), 0)
        c_id = lax.broadcasted_iota(jnp.int32, (T, T), 1)
        diag = jnp.where(r_id == c_id, inter, 0.0)
        col = jnp.sum(diag, axis=1, keepdims=True)
        row = jnp.sum(diag, axis=0, keepdims=True)
        sqc[rows, :] = jnp.broadcast_to(col, (T, 128))
        sqr[:, rows] = jnp.broadcast_to(row, (8, T))
        pred = dot_nt(emb[rows, :], emb[rows, :])
        resid = (pred * norm - inter / (col + row - inter)).astype(BF16)
        return dot_nn(resid, emb[rows, :])

    def cross(upper, lower):
        resid = residual(upper, lower)
        summed[upper, :] += dot_nn(resid, emb[lower, :])
        summed[lower, :] += dot_nn(resid.T, emb[upper, :])

    @pl.loop(0, hidden // T)
    def _(n):
        cols = pl.ds(pl.multiple_of(n * T, T), T)
        encode_columns(pl.ds(0, half), cols)

    @pl.loop(0, d_in // T)
    def _(n):
        cols = pl.ds(pl.multiple_of(n * T, T), T)
        fpt[cols, pl.ds(0, half)] = fp[pl.ds(0, half), cols].T

    embed(pl.ds(0, half), half)
    for r in range(0, half, T):
        summed[pl.ds(r, T), :] = diagonal(pl.ds(r, T))
        if r:
            cross(pl.ds(0, r), pl.ds(r, T))

    @pl.loop(0, pieces)
    def _(p):
        rows = pl.ds(pl.multiple_of(half + p * T, T), T)
        far_copy(p).wait()
        passing(p).start()
        passing(p).wait()
        for n in range(0, hidden, T):
            encode_columns(rows, pl.ds(n, T))
        for n in range(0, d_in, T):
            fpt[pl.ds(n, T), rows] = fp[rows, pl.ds(n, T)].T
        embed(rows, T)
        summed[rows, :] = diagonal(rows)
        cross(pl.ds(0, half), rows)

        @pl.loop(0, p)
        def _(i):
            cross(pl.ds(pl.multiple_of(half + i * T, T), T), rows)

    demb[...] = (summed[...] * scale).astype(BF16)
    quarter = pl.ds(pl.multiple_of(blk * T, T), T)
    for r in range(0, rows_all, 2 * T):
        rows = pl.ds(r, 2 * T)
        back = dot_nt(demb[rows, :], w2[quarter, :])
        dpre[rows, :] = (back * gate[rows, quarter]).astype(BF16)

    def scatter_x(part, out, z0, step):
        sub = step // NX
        for k in range(part.shape[0] // step):
            for xx in range(NX):
                out[xx, pl.ds((z0 + k) * sub, sub), :] = part[
                    k * step + xx * sub : k * step + (xx + 1) * sub
                ].astype(BF16)

    def send_x(src, dst, sems):
        for k in (2, 1, 3):
            to = (x + k) % NX
            copy = remote(
                src(to), dst(k - 1), xs.at[sems, k - 1], xr.at[sems, k - 1], x_peers[k - 1]
            )
            copies.append(copy)
            copy.start()

    copies = []
    for part in range(2):
        span = d_in // 2
        scatter_x(
            dot_nn(fpt[pl.ds(part * span, span), :], dpre[...]),
            xo1, part * NZ // 2, d_in // NZ,
        )
        lines = pl.ds(part * span // NX, span // NX)
        send_x(lambda to: xo1.at[to, lines], lambda k: xb1.at[k, lines], part)
    cols = width // 4
    scatter_x(
        dot_nn(hidt[...], demb[:, pl.ds(pl.multiple_of(blk * cols, cols), cols)]),
        xo2, 0, hidden // NZ,
    )
    send_x(lambda to: xo2.at[to], lambda k: xb2.at[k], 2)
    for copy in copies:
        copy.wait()

    def sum_x(own, buf):
        total = own[x].astype(F32)
        for k in range(NX - 1):
            total = total + buf[k].astype(F32)
        return total

    zs1[...] = sum_x(xo1, xb1).astype(BF16).reshape(zs1.shape)
    zs2[...] = sum_x(xo2, xb2).astype(BF16).reshape(zs2.shape)

    copies = []
    for k in (4, 3, 5, 2, 6, 1, 7):
        peer, to = z_peers[k - 1], (z + k) % NZ
        copies.append(remote(zs1.at[to], zb1.at[k - 1], zs.at[0, k - 1], zr.at[0, k - 1], peer))
        copies.append(remote(zs2.at[to], zb2.at[k - 1], zs.at[1, k - 1], zr.at[1, k - 1], peer))
    for copy in copies:
        copy.start()
    for copy in copies:
        copy.wait()

    def sum_z(own, buf):
        total = own[z].astype(F32)
        for k in range(NZ - 1):
            total = total + buf[k].astype(F32)
        return total

    ys1[...] = sum_z(zs1, zb1).reshape(ys1.shape)
    ys2[...] = sum_z(zs2, zb2).reshape(ys2.shape)

    copies = []
    for k, (dy, dc) in enumerate(y_steps):
        peer, to = y_peers[k], (y + dy) % 2
        slot = y * 2 + c
        copies.append(remote(ys1.at[to], yb1.at[slot], ys.at[0, k], yr.at[0, k], peer))
        copies.append(remote(ys2.at[to], yb2.at[slot], ys.at[1, k], yr.at[1, k], peer))
    for copy in copies:
        copy.start()
    yb1[y * 2 + c] = ys1[y % 2]
    yb2[y * 2 + c] = ys2[y % 2]
    for copy in copies:
        copy.wait()
    for h in range(2):
        for core in range(2):
            q = 2 * h + core
            low, high = 4 * h + core, 4 * h + 2 + core
            o1[:, q * o1.shape[1] // 4 : (q + 1) * o1.shape[1] // 4] = yb1[low] + yb1[high]
            o2[:, q * o2.shape[1] // 4 : (q + 1) * o2.shape[1] // 4] = yb2[low] + yb2[high]


def gradients(fingerprints, w_first, w_second, scale):
    tok, d_in = fingerprints.shape
    hidden, width = w_second.shape
    rows = 4 * tok
    pieces = tok // HALF
    any_spec = pl.BlockSpec(memory_space=pl.ANY)
    vmem_spec = pl.BlockSpec(memory_space=pltpu.VMEM)
    r1, c1 = d_in // NX, hidden // 4
    r2, c2 = hidden // NX, width // 4
    z1, z2 = r1 // NZ, r2 // NZ
    dma = pltpu.SemaphoreType.DMA
    return pl.pallas_call(
        functools.partial(step_kernel, scale),
        out_shape=(
            jax.ShapeDtypeStruct((z1 // 2, 4 * c1), F32),
            jax.ShapeDtypeStruct((z2 // 2, 4 * c2), F32),
        ),
        in_specs=[any_spec] * 3,
        out_specs=(vmem_spec, vmem_spec),
        scratch_shapes=[
            pltpu.VMEM((rows, d_in), BF16),
            pltpu.VMEM((d_in, rows), BF16),
            pltpu.VMEM((d_in, hidden), BF16),
            pltpu.VMEM((hidden, width), BF16),
            pltpu.VMEM((2 * tok, hidden), BF16),
            pltpu.VMEM((hidden, rows), BF16),
            pltpu.VMEM((rows, width), BF16),
            pltpu.VMEM((rows, width), F32),
            pltpu.VMEM((rows, hidden), F32),
            pltpu.VMEM((rows, width), BF16),
            pltpu.VMEM((rows, hidden // 4), BF16),
            pltpu.VMEM((rows, 128), F32),
            pltpu.VMEM((8, rows), F32),
            pltpu.VMEM((NX, r1, c1), BF16),
            pltpu.VMEM((NX, r2, c2), BF16),
            pltpu.VMEM((NX - 1, r1, c1), BF16),
            pltpu.VMEM((NX - 1, r2, c2), BF16),
            pltpu.VMEM((NZ, z1, c1), BF16),
            pltpu.VMEM((NZ, z2, c2), BF16),
            pltpu.VMEM((NZ - 1, z1, c1), BF16),
            pltpu.VMEM((NZ - 1, z2, c2), BF16),
            pltpu.VMEM((2, z1 // 2, c1), F32),
            pltpu.VMEM((2, z2 // 2, c2), F32),
            pltpu.VMEM((8, z1 // 2, c1), F32),
            pltpu.VMEM((8, z2 // 2, c2), F32),
            dma((3,)),
            dma((pieces + 1,)),
            dma((pieces + 1,)),
            dma((pieces,)),
            dma((pieces,)),
            dma((3, NX - 1)),
            dma((3, NX - 1)),
            dma((2, NZ - 1)),
            dma((2, NZ - 1)),
            dma((2, 7)),
            dma((2, 7)),
        ],
        compiler_params=pltpu.CompilerParams(
            collective_id=0, has_side_effects=True, vmem_limit_bytes=60 << 20
        ),
        name="gradients",
    )(fingerprints, w_first, w_second)


def per_device(fingerprints, w_first, w_second):
    group_rows = fingerprints.shape[0] * lax.axis_size("blk")
    all_rows = group_rows * lax.axis_size("dp")
    scale = 2.0 / math.sqrt(group_rows * all_rows)
    return gradients(fingerprints, w_first, w_second, scale)


def solution(mesh):
    in_specs = (P(("blk", "dp"), None), P(), P())
    out_specs = (P("dp", None), P("dp", None))
    return jax.shard_map(
        per_device, mesh=mesh, in_specs=in_specs, out_specs=out_specs, check_vma=False
    )
```

```python
import functools
import math

import jax
import jax.numpy as jnp
from jax import lax
from jax.experimental import pallas as pl
from jax.experimental.pallas import tpu as pltpu
from jax.sharding import PartitionSpec as P

MESH = pl.DeviceIdType.MESH
F32 = jnp.float32
BF16 = jnp.bfloat16
NZ, NX = 8, 4
T = 256
HALF = 128


def dot_nt(a, b):
    return lax.dot_general(a, b, (((1,), (1,)), ((), ())), preferred_element_type=F32)


def dot_nn(a, b):
    return jnp.dot(a, b, preferred_element_type=F32)


def step_kernel(
    scale, fp_in, w1_in, w2_in, o1, o2,
    fp, fpt, w1, w2, hid, hidt, emb, summed, gate, demb, dpre, sqc, sqr,
    gx, rx, gy, ry, gz, rz, hx, qx, hy, qy, hz, qz, kxy, rxy, kz, r3z, f1, r1, f2, r2,
    load_sem, send_sem, recv_sem, pass_send, pass_recv,
    xs, xr, ys, yr, zs, zr, xs2, xr2, ys2, yr2, zs2, zr2, s3, t3, zs3, zr3, s4, t4,
):
    blk = lax.axis_index("blk")
    dp = lax.axis_index("dp")
    z, x = dp // 8, (dp // 2) % 4
    y, c = (blk // 2) * 2 + dp % 2, blk % 2
    tok, d_in = fp_in.shape
    hidden, width = w2_in.shape
    half = 2 * tok
    rows_all = 4 * tok
    pieces = tok // HALF
    norm = 1.0 / math.sqrt(width)

    def at(z, x, y, c):
        return {"blk": (y // 2) * 2 + c, "dp": (z * NX + x) * 2 + y % 2}

    side = y % 2
    far = at(z, x, (y + 2) % 4, c)
    near = at(z, x, y, 1 - c)
    cross_far = at(z, x, (y + 2) % 4, 1 - c)
    pair = at(z, x, (y // 2) * 2 + 1 - side, c)
    x_peers = [at(z, (x + k) % NX, y, c) for k in range(1, NX)]
    z_peers = [at((z + k) % NZ, x, y, c) for k in range(1, NZ)]
    peers = [far, near, cross_far, pair] + x_peers + z_peers

    barrier = pltpu.get_barrier_semaphore()
    for peer in peers:
        pl.semaphore_signal(barrier, inc=1, device_id=peer, device_id_type=MESH)
    loads = [
        pltpu.make_async_copy(fp_in, fp.at[pl.ds(0, tok)], load_sem.at[0]),
        pltpu.make_async_copy(w1_in, w1, load_sem.at[1]),
        pltpu.make_async_copy(w2_in, w2, load_sem.at[2]),
    ]
    for load in loads:
        load.start()
    pl.semaphore_wait(barrier, len(peers))

    def remote(src, dst, send, recv, peer):
        return pltpu.make_async_remote_copy(
            src_ref=src, dst_ref=dst, send_sem=send, recv_sem=recv,
            device_id=peer, device_id_type=MESH,
        )

    def far_copy(p):
        return remote(
            fp_in.at[pl.ds(p * HALF, HALF)], fp.at[pl.ds(half + p * T, HALF)],
            send_sem.at[p], recv_sem.at[p], far,
        )

    def passing(p):
        return remote(
            fp.at[pl.ds(half + p * T, HALF)], fp.at[pl.ds(half + p * T + HALF, HALF)],
            pass_send.at[p], pass_recv.at[p], near,
        )

    near_copy = remote(
        fp_in, fp.at[pl.ds(tok, tok)], send_sem.at[pieces], recv_sem.at[pieces], near
    )
    for p in range(pieces):
        far_copy(p).start()
    near_copy.start()
    for load in loads:
        load.wait()
    near_copy.wait()

    def encode_columns(rows, cols):
        pre = dot_nn(fp[rows, :], w1[:, cols])
        sig = 1.0 / (1.0 + jnp.exp(-pre))
        h = (pre * sig).astype(BF16)
        hid[pl.ds(0, h.shape[0]), cols] = h
        hidt[cols, rows] = h.T
        gate[rows, cols] = sig * (1.0 + pre * (1.0 - sig))

    def embed(rows, count):
        emb[rows, :] = dot_nn(hid[pl.ds(0, count), :], w2[...]).astype(BF16)

    def residual(upper, lower):
        inter = dot_nt(fp[upper, :], fp[lower, :])
        den = sqc[upper, :][:, :1] + sqr[:1, lower] - inter
        pred = dot_nt(emb[upper, :], emb[lower, :])
        return (pred * norm - inter / den).astype(BF16)

    def diagonal(rows):
        inter = dot_nt(fp[rows, :], fp[rows, :])
        r_id = lax.broadcasted_iota(jnp.int32, (T, T), 0)
        c_id = lax.broadcasted_iota(jnp.int32, (T, T), 1)
        diag = jnp.where(r_id == c_id, inter, 0.0)
        col = jnp.sum(diag, axis=1, keepdims=True)
        row = jnp.sum(diag, axis=0, keepdims=True)
        sqc[rows, :] = jnp.broadcast_to(col, (T, 128))
        sqr[:, rows] = jnp.broadcast_to(row, (8, T))
        pred = dot_nt(emb[rows, :], emb[rows, :])
        resid = (pred * norm - inter / (col + row - inter)).astype(BF16)
        return dot_nn(resid, emb[rows, :])

    def cross(upper, lower):
        resid = residual(upper, lower)
        summed[upper, :] += dot_nn(resid, emb[lower, :])
        summed[lower, :] += dot_nn(resid.T, emb[upper, :])

    @pl.loop(0, hidden // T)
    def _(n):
        cols = pl.ds(pl.multiple_of(n * T, T), T)
        encode_columns(pl.ds(0, half), cols)

    @pl.loop(0, d_in // T)
    def _(n):
        cols = pl.ds(pl.multiple_of(n * T, T), T)
        fpt[cols, pl.ds(0, half)] = fp[pl.ds(0, half), cols].T

    embed(pl.ds(0, half), half)
    for r in range(0, half, T):
        summed[pl.ds(r, T), :] = diagonal(pl.ds(r, T))
        if r:
            cross(pl.ds(0, r), pl.ds(r, T))

    @pl.loop(0, pieces)
    def _(p):
        rows = pl.ds(pl.multiple_of(half + p * T, T), T)
        far_copy(p).wait()
        passing(p).start()
        passing(p).wait()
        for n in range(0, hidden, T):
            encode_columns(rows, pl.ds(n, T))
        for n in range(0, d_in, T):
            fpt[pl.ds(n, T), rows] = fp[rows, pl.ds(n, T)].T
        embed(rows, T)
        summed[rows, :] = diagonal(rows)
        cross(pl.ds(0, half), rows)

        @pl.loop(0, p)
        def _(i):
            cross(pl.ds(pl.multiple_of(half + i * T, T), T), rows)

    demb[...] = (summed[...] * scale).astype(BF16)
    cols = width // 4
    part = dot_nn(hidt[...], demb[:, pl.ds(pl.multiple_of(blk * cols, cols), cols)])
    gz[...] = part.astype(BF16).reshape(gz.shape)
    z_copies = [
        remote(gz.at[(z + k) % NZ], rz.at[k - 1], zs.at[k - 1], zr.at[k - 1], z_peers[k - 1])
        for k in (4, 3, 5, 2, 6, 1, 7)
    ]
    for copy in z_copies:
        copy.start()

    quarter = pl.ds(pl.multiple_of(blk * T, T), T)
    for r in range(0, rows_all, 2 * T):
        rows = pl.ds(r, 2 * T)
        back = dot_nt(demb[rows, :], w2[quarter, :])
        dpre[rows, :] = (back * gate[rows, quarter]).astype(BF16)

    x_copies, y_copies = [], []
    span = NZ // 2
    own = gy.shape[3]
    for i in range(2):
        rows = pl.ds(i * d_in // 2, d_in // 2)
        part = dot_nn(fpt[rows, :], dpre[...]).astype(BF16)
        for k in range(span):
            zz = i * span + k
            for xx in range(NX):
                for ll in range(2):
                    line = ((k * NX + xx) * 2 + ll) * own
                    gx[xx, zz, ll * own : (ll + 1) * own, :] = part[line : line + own, :128]
                    gy[ll, zz, xx] = part[line : line + own, 128:]
        zz = pl.ds(i * span, span)
        copy = remote(gy.at[1 - side, zz], ry.at[zz], ys.at[i], yr.at[i], pair)
        y_copies.append(copy)
        copy.start()
        for k in (2, 1, 3):
            copy = remote(
                gx.at[(x + k) % NX, zz], rx.at[k - 1, zz],
                xs.at[i, k - 1], xr.at[i, k - 1], x_peers[k - 1],
            )
            x_copies.append(copy)
            copy.start()

    def total(mine, others):
        out = mine.astype(F32)
        for k in range(others.shape[0]):
            out = out + others[k].astype(F32)
        return out

    for copy in y_copies:
        copy.wait()
    for xx in range(NX):
        hy[xx] = (gy[side, :, xx].astype(F32) + ry[:, xx].astype(F32)).astype(BF16)
    y_copies = [
        remote(hy.at[(x + k) % NX], qy.at[k - 1], ys2.at[k - 1], yr2.at[k - 1], x_peers[k - 1])
        for k in (2, 1, 3)
    ]
    for copy in y_copies:
        copy.start()

    for copy in x_copies:
        copy.wait()
    part = total(gx[x], rx).astype(BF16)
    for ll in range(2):
        hx[ll] = part[:, ll * own : (ll + 1) * own, :]
    x_copy = remote(hx.at[1 - side], qx, xs2, xr2, pair)
    x_copy.start()

    for copy in z_copies:
        copy.wait()
    hz[...] = total(gz[z], rz).astype(BF16).reshape(hz.shape)
    z_copies = [
        remote(hz.at[(x + k) % NX], qz.at[k - 1], zs2.at[k - 1], zr2.at[k - 1], x_peers[k - 1])
        for k in (2, 1, 3)
    ]
    for copy in z_copies:
        copy.start()

    x_copy.wait()
    kxy[:, :, :128] = (hx[side].astype(F32) + qx[...].astype(F32)).astype(BF16)
    for copy in y_copies:
        copy.wait()
    kxy[:, :, 128:] = total(hy[x], qy).astype(BF16)
    copies = [
        remote(kxy.at[(z + k) % NZ], rxy.at[k - 1], s3.at[k - 1], t3.at[k - 1], z_peers[k - 1])
        for k in (4, 3, 5, 2, 6, 1, 7)
    ]
    for copy in copies:
        copy.start()

    for copy in z_copies:
        copy.wait()
    kz[...] = total(hz[x], qz).reshape(kz.shape)
    z_copy = remote(kz.at[1 - side], r3z, zs3, zr3, pair)
    z_copy.start()
    z_copy.wait()
    f2[...] = kz[side] + r3z[...]

    def spread(src, dst, i):
        out = [
            remote(src, dst.at[blk], s4.at[i, k], t4.at[i, k], peer)
            for k, peer in enumerate((cross_far, far, near))
        ]
        for copy in out:
            copy.start()
        return out

    last = spread(f2, r2, 0)
    for copy in copies:
        copy.wait()
    f1[...] = total(kxy[z], rxy)
    last += spread(f1, r1, 1)
    r1[blk] = f1[...]
    r2[blk] = f2[...]
    for copy in last:
        copy.wait()
    for q in range(4):
        o1[:, q * o1.shape[1] // 4 : (q + 1) * o1.shape[1] // 4] = r1[q]
        o2[:, q * o2.shape[1] // 4 : (q + 1) * o2.shape[1] // 4] = r2[q]


def gradients(fingerprints, w_first, w_second, scale):
    tok, d_in = fingerprints.shape
    hidden, width = w_second.shape
    rows = 4 * tok
    pieces = tok // HALF
    any_spec = pl.BlockSpec(memory_space=pl.ANY)
    vmem_spec = pl.BlockSpec(memory_space=pltpu.VMEM)
    c1, c2 = hidden // 4, width // 4
    n1, n2 = d_in // (NZ * NX * 2), hidden // (NZ * NX * 2)
    dma = pltpu.SemaphoreType.DMA
    return pl.pallas_call(
        functools.partial(step_kernel, scale),
        out_shape=(
            jax.ShapeDtypeStruct((n1, 4 * c1), F32),
            jax.ShapeDtypeStruct((n2, 4 * c2), F32),
        ),
        in_specs=[any_spec] * 3,
        out_specs=(vmem_spec, vmem_spec),
        scratch_shapes=[
            pltpu.VMEM((rows, d_in), BF16),
            pltpu.VMEM((d_in, rows), BF16),
            pltpu.VMEM((d_in, hidden), BF16),
            pltpu.VMEM((hidden, width), BF16),
            pltpu.VMEM((2 * tok, hidden), BF16),
            pltpu.VMEM((hidden, rows), BF16),
            pltpu.VMEM((rows, width), BF16),
            pltpu.VMEM((rows, width), F32),
            pltpu.VMEM((rows, hidden), F32),
            pltpu.VMEM((rows, width), BF16),
            pltpu.VMEM((rows, hidden // 4), BF16),
            pltpu.VMEM((rows, 128), F32),
            pltpu.VMEM((8, rows), F32),
            pltpu.VMEM((NX, NZ, 2 * n1, 128), BF16),
            pltpu.VMEM((NX - 1, NZ, 2 * n1, 128), BF16),
            pltpu.VMEM((2, NZ, NX, n1, 128), BF16),
            pltpu.VMEM((NZ, NX, n1, 128), BF16),
            pltpu.VMEM((NZ, NX * 2 * n2, c2), BF16),
            pltpu.VMEM((NZ - 1, NX * 2 * n2, c2), BF16),
            pltpu.VMEM((2, NZ, n1, 128), BF16),
            pltpu.VMEM((NZ, n1, 128), BF16),
            pltpu.VMEM((NX, NZ, n1, 128), BF16),
            pltpu.VMEM((NX - 1, NZ, n1, 128), BF16),
            pltpu.VMEM((NX, 2 * n2, c2), BF16),
            pltpu.VMEM((NX - 1, 2 * n2, c2), BF16),
            pltpu.VMEM((NZ, n1, c1), BF16),
            pltpu.VMEM((NZ - 1, n1, c1), BF16),
            pltpu.VMEM((2, n2, c2), F32),
            pltpu.VMEM((n2, c2), F32),
            pltpu.VMEM((n1, c1), F32),
            pltpu.VMEM((4, n1, c1), F32),
            pltpu.VMEM((n2, c2), F32),
            pltpu.VMEM((4, n2, c2), F32),
            dma((3,)),
            dma((pieces + 1,)),
            dma((pieces + 1,)),
            dma((pieces,)),
            dma((pieces,)),
            dma((2, NX - 1)),
            dma((2, NX - 1)),
            dma((2,)),
            dma((2,)),
            dma((NZ - 1,)),
            dma((NZ - 1,)),
            dma,
            dma,
            dma((NX - 1,)),
            dma((NX - 1,)),
            dma((NX - 1,)),
            dma((NX - 1,)),
            dma((NZ - 1,)),
            dma((NZ - 1,)),
            dma,
            dma,
            dma((2, 3)),
            dma((2, 3)),
        ],
        compiler_params=pltpu.CompilerParams(
            collective_id=0, has_side_effects=True, vmem_limit_bytes=60 << 20
        ),
        name="gradients",
    )(fingerprints, w_first, w_second)


def per_device(fingerprints, w_first, w_second):
    group_rows = fingerprints.shape[0] * lax.axis_size("blk")
    all_rows = group_rows * lax.axis_size("dp")
    scale = 2.0 / math.sqrt(group_rows * all_rows)
    return gradients(fingerprints, w_first, w_second, scale)


def solution(mesh):
    in_specs = (P(("blk", "dp"), None), P(), P())
    out_specs = (P("dp", None), P("dp", None))
    return jax.shard_map(
        per_device, mesh=mesh, in_specs=in_specs, out_specs=out_specs, check_vma=False
    )
```

```python
import functools
import math

import jax
import jax.numpy as jnp
from jax import lax
from jax.experimental import pallas as pl
from jax.experimental.pallas import tpu as pltpu
from jax.sharding import PartitionSpec as P

MESH = pl.DeviceIdType.MESH
F32 = jnp.float32
BF16 = jnp.bfloat16
NZ, NX = 8, 4
T = 256
HALF = 128


def dot_nt(a, b):
    return lax.dot_general(a, b, (((1,), (1,)), ((), ())), preferred_element_type=F32)


def dot_nn(a, b):
    return jnp.dot(a, b, preferred_element_type=F32)


def step_kernel(
    scale, fp_in, w1_in, w2_in, o1, o2,
    fp, fpt, w1, w2, hid, hidt, emb, summed, gate, demb, dpre, sqc, sqr,
    gx, rx, gy, ry, gz, rz, hx, qx, hy, qy, hz, qz, kx, r3x, ky, qky, kz, r3z, f1, r1, f2, r2,
    load_sem, send_sem, recv_sem, pass_send, pass_recv,
    xs, xr, ys, yr, zs, zr, xs2, xr2, ys2, yr2, zs2, zr2, xs3, xr3, s3, t3, zs3, zr3, s4, t4,
):
    blk = lax.axis_index("blk")
    dp = lax.axis_index("dp")
    z, x = dp // 8, (dp // 2) % 4
    y, c = (blk // 2) * 2 + dp % 2, blk % 2
    tok, d_in = fp_in.shape
    hidden, width = w2_in.shape
    half = 2 * tok
    rows_all = 4 * tok
    pieces = tok // HALF
    norm = 1.0 / math.sqrt(width)

    def at(z, x, y, c):
        return {"blk": (y // 2) * 2 + c, "dp": (z * NX + x) * 2 + y % 2}

    side = y % 2
    far = at(z, x, (y + 2) % 4, c)
    near = at(z, x, y, 1 - c)
    cross_far = at(z, x, (y + 2) % 4, 1 - c)
    pair = at(z, x, (y // 2) * 2 + 1 - side, c)
    x_peers = [at(z, (x + k) % NX, y, c) for k in range(1, NX)]
    z_peers = [at((z + k) % NZ, x, y, c) for k in range(1, NZ)]
    peers = [far, near, cross_far, pair] + x_peers + z_peers

    barrier = pltpu.get_barrier_semaphore()
    for peer in peers:
        pl.semaphore_signal(barrier, inc=1, device_id=peer, device_id_type=MESH)
    loads = [
        pltpu.make_async_copy(fp_in, fp.at[pl.ds(0, tok)], load_sem.at[0]),
        pltpu.make_async_copy(w1_in, w1, load_sem.at[1]),
        pltpu.make_async_copy(w2_in, w2, load_sem.at[2]),
    ]
    for load in loads:
        load.start()
    pl.semaphore_wait(barrier, len(peers))

    def remote(src, dst, send, recv, peer):
        return pltpu.make_async_remote_copy(
            src_ref=src, dst_ref=dst, send_sem=send, recv_sem=recv,
            device_id=peer, device_id_type=MESH,
        )

    def far_copy(p):
        return remote(
            fp_in.at[pl.ds(p * HALF, HALF)], fp.at[pl.ds(half + p * T, HALF)],
            send_sem.at[p], recv_sem.at[p], far,
        )

    def passing(p):
        return remote(
            fp.at[pl.ds(half + p * T, HALF)], fp.at[pl.ds(half + p * T + HALF, HALF)],
            pass_send.at[p], pass_recv.at[p], near,
        )

    near_copy = remote(
        fp_in, fp.at[pl.ds(tok, tok)], send_sem.at[pieces], recv_sem.at[pieces], near
    )
    for p in range(pieces):
        far_copy(p).start()
    near_copy.start()
    for load in loads:
        load.wait()
    near_copy.wait()

    def encode_columns(rows, cols):
        pre = dot_nn(fp[rows, :], w1[:, cols])
        sig = 1.0 / (1.0 + jnp.exp(-pre))
        h = (pre * sig).astype(BF16)
        hid[pl.ds(0, h.shape[0]), cols] = h
        hidt[cols, rows] = h.T
        gate[rows, cols] = sig * (1.0 + pre * (1.0 - sig))

    def embed(rows, count):
        emb[rows, :] = dot_nn(hid[pl.ds(0, count), :], w2[...]).astype(BF16)

    def residual(upper, lower):
        inter = dot_nt(fp[upper, :], fp[lower, :])
        den = sqc[upper, :][:, :1] + sqr[:1, lower] - inter
        pred = dot_nt(emb[upper, :], emb[lower, :])
        return (pred * norm - inter / den).astype(BF16)

    def diagonal(rows):
        inter = dot_nt(fp[rows, :], fp[rows, :])
        r_id = lax.broadcasted_iota(jnp.int32, (T, T), 0)
        c_id = lax.broadcasted_iota(jnp.int32, (T, T), 1)
        diag = jnp.where(r_id == c_id, inter, 0.0)
        col = jnp.sum(diag, axis=1, keepdims=True)
        row = jnp.sum(diag, axis=0, keepdims=True)
        sqc[rows, :] = jnp.broadcast_to(col, (T, 128))
        sqr[:, rows] = jnp.broadcast_to(row, (8, T))
        pred = dot_nt(emb[rows, :], emb[rows, :])
        resid = (pred * norm - inter / (col + row - inter)).astype(BF16)
        return dot_nn(resid, emb[rows, :])

    def cross(upper, lower):
        resid = residual(upper, lower)
        summed[upper, :] += dot_nn(resid, emb[lower, :])
        summed[lower, :] += dot_nn(resid.T, emb[upper, :])

    @pl.loop(0, hidden // T)
    def _(n):
        cols = pl.ds(pl.multiple_of(n * T, T), T)
        encode_columns(pl.ds(0, half), cols)

    @pl.loop(0, d_in // T)
    def _(n):
        cols = pl.ds(pl.multiple_of(n * T, T), T)
        fpt[cols, pl.ds(0, half)] = fp[pl.ds(0, half), cols].T

    embed(pl.ds(0, half), half)
    for r in range(0, half, T):
        summed[pl.ds(r, T), :] = diagonal(pl.ds(r, T))
        if r:
            cross(pl.ds(0, r), pl.ds(r, T))

    @pl.loop(0, pieces)
    def _(p):
        rows = pl.ds(pl.multiple_of(half + p * T, T), T)
        far_copy(p).wait()
        passing(p).start()
        passing(p).wait()
        for n in range(0, hidden, T):
            encode_columns(rows, pl.ds(n, T))
        for n in range(0, d_in, T):
            fpt[pl.ds(n, T), rows] = fp[rows, pl.ds(n, T)].T
        embed(rows, T)
        summed[rows, :] = diagonal(rows)
        cross(pl.ds(0, half), rows)

        @pl.loop(0, p)
        def _(i):
            cross(pl.ds(pl.multiple_of(half + i * T, T), T), rows)

    demb[...] = (summed[...] * scale).astype(BF16)
    cols = width // 4
    part = dot_nn(hidt[...], demb[:, pl.ds(pl.multiple_of(blk * cols, cols), cols)])
    gz[...] = part.astype(BF16).reshape(gz.shape)
    z_copies = [
        remote(gz.at[(z + k) % NZ], rz.at[k - 1], zs.at[k - 1], zr.at[k - 1], z_peers[k - 1])
        for k in (4, 3, 5, 2, 6, 1, 7)
    ]
    for copy in z_copies:
        copy.start()

    quarter = pl.ds(pl.multiple_of(blk * T, T), T)
    for r in range(0, rows_all, 2 * T):
        rows = pl.ds(r, 2 * T)
        back = dot_nt(demb[rows, :], w2[quarter, :])
        dpre[rows, :] = (back * gate[rows, quarter]).astype(BF16)

    x_copies, y_copies = [], []
    span = NZ // 2
    own = gy.shape[3]
    for i in range(2):
        rows = pl.ds(i * d_in // 2, d_in // 2)
        part = dot_nn(fpt[rows, :], dpre[...]).astype(BF16)
        for k in range(span):
            zz = i * span + k
            for xx in range(NX):
                for ll in range(2):
                    line = ((k * NX + xx) * 2 + ll) * own
                    gx[xx, zz, ll * own : (ll + 1) * own, :] = part[line : line + own, :128]
                    gy[ll, zz, xx] = part[line : line + own, 128:]
        zz = pl.ds(i * span, span)
        copy = remote(gy.at[1 - side, zz], ry.at[zz], ys.at[i], yr.at[i], pair)
        y_copies.append(copy)
        copy.start()
        for k in (2, 1, 3):
            copy = remote(
                gx.at[(x + k) % NX, zz], rx.at[k - 1, zz],
                xs.at[i, k - 1], xr.at[i, k - 1], x_peers[k - 1],
            )
            x_copies.append(copy)
            copy.start()

    def total(mine, others):
        out = mine.astype(F32)
        for k in range(others.shape[0]):
            out = out + others[k].astype(F32)
        return out

    for copy in y_copies:
        copy.wait()
    for xx in range(NX):
        hy[xx] = (gy[side, :, xx].astype(F32) + ry[:, xx].astype(F32)).astype(BF16)
    y_copies = [
        remote(hy.at[(x + k) % NX], qy.at[k - 1], ys2.at[k - 1], yr2.at[k - 1], x_peers[k - 1])
        for k in (2, 1, 3)
    ]
    for copy in y_copies:
        copy.start()

    for copy in x_copies:
        copy.wait()
    hx[...] = total(gx[x], rx).astype(BF16)
    x_copies = [
        remote(hx.at[(z + k) % NZ], qx.at[k - 1], xs2.at[k - 1], xr2.at[k - 1], z_peers[k - 1])
        for k in (4, 3, 5, 2, 6, 1, 7)
    ]
    for copy in x_copies:
        copy.start()

    for copy in z_copies:
        copy.wait()
    hz[...] = total(gz[z], rz).reshape(hz.shape)
    z_copies = [
        remote(hz.at[(x + k) % NX], qz.at[k - 1], zs2.at[k - 1], zr2.at[k - 1], x_peers[k - 1])
        for k in (2, 1, 3)
    ]
    for copy in z_copies:
        copy.start()

    for copy in y_copies:
        copy.wait()
    ky[...] = total(hy[x], qy)
    copies = [
        remote(ky.at[(z + k) % NZ], qky.at[k - 1], s3.at[k - 1], t3.at[k - 1], z_peers[k - 1])
        for k in (4, 3, 5, 2, 6, 1, 7)
    ]
    for copy in copies:
        copy.start()

    for copy in z_copies:
        copy.wait()
    kz[...] = total(hz[x], qz).reshape(kz.shape)
    z_copy = remote(kz.at[1 - side], r3z, zs3, zr3, pair)
    z_copy.start()
    for copy in x_copies:
        copy.wait()
    kx[...] = total(hx[z], qx).reshape(kx.shape)
    x_copy = remote(kx.at[1 - side], r3x, xs3, xr3, pair)
    x_copy.start()
    z_copy.wait()
    f2[...] = kz[side] + r3z[...]

    def spread(src, dst, i):
        out = [
            remote(src, dst.at[blk], s4.at[i, k], t4.at[i, k], peer)
            for k, peer in enumerate((cross_far, far, near))
        ]
        for copy in out:
            copy.start()
        return out

    last = spread(f2, r2, 0)
    x_copy.wait()
    f1[:, :128] = kx[side] + r3x[...]
    for copy in copies:
        copy.wait()
    f1[:, 128:] = total(ky[z], qky)
    last += spread(f1, r1, 1)
    r1[blk] = f1[...]
    r2[blk] = f2[...]
    for copy in last:
        copy.wait()
    for q in range(4):
        o1[:, q * o1.shape[1] // 4 : (q + 1) * o1.shape[1] // 4] = r1[q]
        o2[:, q * o2.shape[1] // 4 : (q + 1) * o2.shape[1] // 4] = r2[q]


def gradients(fingerprints, w_first, w_second, scale):
    tok, d_in = fingerprints.shape
    hidden, width = w_second.shape
    rows = 4 * tok
    pieces = tok // HALF
    any_spec = pl.BlockSpec(memory_space=pl.ANY)
    vmem_spec = pl.BlockSpec(memory_space=pltpu.VMEM)
    c1, c2 = hidden // 4, width // 4
    n1, n2 = d_in // (NZ * NX * 2), hidden // (NZ * NX * 2)
    dma = pltpu.SemaphoreType.DMA
    return pl.pallas_call(
        functools.partial(step_kernel, scale),
        out_shape=(
            jax.ShapeDtypeStruct((n1, 4 * c1), F32),
            jax.ShapeDtypeStruct((n2, 4 * c2), F32),
        ),
        in_specs=[any_spec] * 3,
        out_specs=(vmem_spec, vmem_spec),
        scratch_shapes=[
            pltpu.VMEM((rows, d_in), BF16),
            pltpu.VMEM((d_in, rows), BF16),
            pltpu.VMEM((d_in, hidden), BF16),
            pltpu.VMEM((hidden, width), BF16),
            pltpu.VMEM((2 * tok, hidden), BF16),
            pltpu.VMEM((hidden, rows), BF16),
            pltpu.VMEM((rows, width), BF16),
            pltpu.VMEM((rows, width), F32),
            pltpu.VMEM((rows, hidden), F32),
            pltpu.VMEM((rows, width), BF16),
            pltpu.VMEM((rows, hidden // 4), BF16),
            pltpu.VMEM((rows, 128), F32),
            pltpu.VMEM((8, rows), F32),
            pltpu.VMEM((NX, NZ, 2 * n1, 128), BF16),
            pltpu.VMEM((NX - 1, NZ, 2 * n1, 128), BF16),
            pltpu.VMEM((2, NZ, NX, n1, 128), BF16),
            pltpu.VMEM((NZ, NX, n1, 128), BF16),
            pltpu.VMEM((NZ, NX * 2 * n2, c2), BF16),
            pltpu.VMEM((NZ - 1, NX * 2 * n2, c2), BF16),
            pltpu.VMEM((NZ, 2 * n1, 128), BF16),
            pltpu.VMEM((NZ - 1, 2 * n1, 128), BF16),
            pltpu.VMEM((NX, NZ, n1, 128), BF16),
            pltpu.VMEM((NX - 1, NZ, n1, 128), BF16),
            pltpu.VMEM((NX, 2 * n2, c2), F32),
            pltpu.VMEM((NX - 1, 2 * n2, c2), F32),
            pltpu.VMEM((2, n1, 128), F32),
            pltpu.VMEM((n1, 128), F32),
            pltpu.VMEM((NZ, n1, 128), F32),
            pltpu.VMEM((NZ - 1, n1, 128), F32),
            pltpu.VMEM((2, n2, c2), F32),
            pltpu.VMEM((n2, c2), F32),
            pltpu.VMEM((n1, c1), F32),
            pltpu.VMEM((4, n1, c1), F32),
            pltpu.VMEM((n2, c2), F32),
            pltpu.VMEM((4, n2, c2), F32),
            dma((3,)),
            dma((pieces + 1,)),
            dma((pieces + 1,)),
            dma((pieces,)),
            dma((pieces,)),
            dma((2, NX - 1)),
            dma((2, NX - 1)),
            dma((2,)),
            dma((2,)),
            dma((NZ - 1,)),
            dma((NZ - 1,)),
            dma((NZ - 1,)),
            dma((NZ - 1,)),
            dma((NX - 1,)),
            dma((NX - 1,)),
            dma((NX - 1,)),
            dma((NX - 1,)),
            dma,
            dma,
            dma((NZ - 1,)),
            dma((NZ - 1,)),
            dma,
            dma,
            dma((2, 3)),
            dma((2, 3)),
        ],
        compiler_params=pltpu.CompilerParams(
            collective_id=0, has_side_effects=True, vmem_limit_bytes=60 << 20
        ),
        name="gradients",
    )(fingerprints, w_first, w_second)


def per_device(fingerprints, w_first, w_second):
    group_rows = fingerprints.shape[0] * lax.axis_size("blk")
    all_rows = group_rows * lax.axis_size("dp")
    scale = 2.0 / math.sqrt(group_rows * all_rows)
    return gradients(fingerprints, w_first, w_second, scale)


def solution(mesh):
    in_specs = (P(("blk", "dp"), None), P(), P())
    out_specs = (P("dp", None), P("dp", None))
    return jax.shard_map(
        per_device, mesh=mesh, in_specs=in_specs, out_specs=out_specs, check_vma=False
    )
```

```python
import functools
import math

import jax
import jax.numpy as jnp
from jax import lax
from jax.experimental import pallas as pl
from jax.experimental.pallas import tpu as pltpu
from jax.sharding import PartitionSpec as P

MESH = pl.DeviceIdType.MESH
F32 = jnp.float32
BF16 = jnp.bfloat16
NZ, NX = 8, 4
T = 256
SPLIT = (3, 2, 1)


def dot_nt(a, b):
    return lax.dot_general(a, b, (((1,), (1,)), ((), ())), preferred_element_type=F32)


def dot_nn(a, b):
    return jnp.dot(a, b, preferred_element_type=F32)


def step_kernel(
    scale, fp_in, w1_in, w2_in, o1, o2,
    fp, fpt, w1, w2, hid, hidt, emb, summed, gate, demb, dpre, sqc, sqr,
    gx, rx, gy, ry, gz, rz, hx, qx, hy, qy, hz, qz, kx, r3x, ky, qky, kz, r3z, f1, r1, f2, r2,
    load_sem, send_sem, recv_sem, pass_send, pass_recv,
    xs, xr, ys, yr, zs, zr, xs2, xr2, ys2, yr2, zs2, zr2, xs3, xr3, s3, t3, zs3, zr3, s4, t4,
):
    blk = lax.axis_index("blk")
    dp = lax.axis_index("dp")
    z, x = dp // 8, (dp // 2) % 4
    y, c = (blk // 2) * 2 + dp % 2, blk % 2
    tok, d_in = fp_in.shape
    hidden, width = w2_in.shape
    half = 2 * tok
    rows_all = 4 * tok
    pieces = len(SPLIT)
    sizes = [tok * share // sum(SPLIT) for share in SPLIT]
    firsts = [sum(sizes[:p]) for p in range(pieces)]
    norm = 1.0 / math.sqrt(width)

    def at(z, x, y, c):
        return {"blk": (y // 2) * 2 + c, "dp": (z * NX + x) * 2 + y % 2}

    side = y % 2
    far = at(z, x, (y + 2) % 4, c)
    near = at(z, x, y, 1 - c)
    cross_far = at(z, x, (y + 2) % 4, 1 - c)
    pair = at(z, x, (y // 2) * 2 + 1 - side, c)
    x_peers = [at(z, (x + k) % NX, y, c) for k in range(1, NX)]
    z_peers = [at((z + k) % NZ, x, y, c) for k in range(1, NZ)]
    peers = [far, near, cross_far, pair] + x_peers + z_peers

    barrier = pltpu.get_barrier_semaphore()
    for peer in peers:
        pl.semaphore_signal(barrier, inc=1, device_id=peer, device_id_type=MESH)
    loads = [
        pltpu.make_async_copy(fp_in, fp.at[pl.ds(0, tok)], load_sem.at[0]),
        pltpu.make_async_copy(w1_in, w1, load_sem.at[1]),
        pltpu.make_async_copy(w2_in, w2, load_sem.at[2]),
    ]
    for load in loads:
        load.start()
    pl.semaphore_wait(barrier, len(peers))

    def remote(src, dst, send, recv, peer):
        return pltpu.make_async_remote_copy(
            src_ref=src, dst_ref=dst, send_sem=send, recv_sem=recv,
            device_id=peer, device_id_type=MESH,
        )

    def far_copy(p):
        return remote(
            fp_in.at[pl.ds(firsts[p], sizes[p])],
            fp.at[pl.ds(half + 2 * firsts[p], sizes[p])],
            send_sem.at[p], recv_sem.at[p], far,
        )

    def passing(p):
        return remote(
            fp.at[pl.ds(half + 2 * firsts[p], sizes[p])],
            fp.at[pl.ds(half + 2 * firsts[p] + sizes[p], sizes[p])],
            pass_send.at[p], pass_recv.at[p], near,
        )

    near_copy = remote(
        fp_in, fp.at[pl.ds(tok, tok)], send_sem.at[pieces], recv_sem.at[pieces], near
    )
    for p in range(pieces):
        far_copy(p).start()
    near_copy.start()
    for load in loads:
        load.wait()
    near_copy.wait()

    def encode_columns(rows, cols):
        pre = dot_nn(fp[rows, :], w1[:, cols])
        sig = 1.0 / (1.0 + jnp.exp(-pre))
        h = (pre * sig).astype(BF16)
        hid[pl.ds(0, h.shape[0]), cols] = h
        hidt[cols, rows] = h.T
        gate[rows, cols] = sig * (1.0 + pre * (1.0 - sig))

    def embed(rows, count):
        emb[rows, :] = dot_nn(hid[pl.ds(0, count), :], w2[...]).astype(BF16)

    def residual(upper, lower):
        inter = dot_nt(fp[upper, :], fp[lower, :])
        den = sqc[upper, :][:, :1] + sqr[:1, lower] - inter
        pred = dot_nt(emb[upper, :], emb[lower, :])
        return (pred * norm - inter / den).astype(BF16)

    def diagonal(first, count):
        rows = pl.ds(first, count)
        inter = dot_nt(fp[rows, :], fp[rows, :])
        r_id = lax.broadcasted_iota(jnp.int32, (count, count), 0)
        c_id = lax.broadcasted_iota(jnp.int32, (count, count), 1)
        diag = jnp.where(r_id == c_id, inter, 0.0)
        col = jnp.sum(diag, axis=1, keepdims=True)
        row = jnp.sum(diag, axis=0, keepdims=True)
        sqc[rows, :] = jnp.broadcast_to(col, (count, 128))
        sqr[:, rows] = jnp.broadcast_to(row, (8, count))
        pred = dot_nt(emb[rows, :], emb[rows, :])
        resid = (pred * norm - inter / (col + row - inter)).astype(BF16)
        summed[rows, :] = dot_nn(resid, emb[rows, :])

    def cross(upper, lower):
        resid = residual(upper, lower)
        summed[upper, :] += dot_nn(resid, emb[lower, :])
        summed[lower, :] += dot_nn(resid.T, emb[upper, :])

    @pl.loop(0, hidden // T)
    def _(n):
        cols = pl.ds(pl.multiple_of(n * T, T), T)
        encode_columns(pl.ds(0, half), cols)

    @pl.loop(0, d_in // T)
    def _(n):
        cols = pl.ds(pl.multiple_of(n * T, T), T)
        fpt[cols, pl.ds(0, half)] = fp[pl.ds(0, half), cols].T

    embed(pl.ds(0, half), half)
    for r in range(0, half, T):
        diagonal(r, T)
        if r:
            cross(pl.ds(0, r), pl.ds(r, T))

    for p in range(pieces):
        first, count = half + 2 * firsts[p], 2 * sizes[p]
        rows = pl.ds(first, count)
        far_copy(p).wait()
        passing(p).start()
        passing(p).wait()
        for n in range(0, hidden, T):
            encode_columns(rows, pl.ds(n, T))
        for n in range(0, d_in, T):
            fpt[pl.ds(n, T), rows] = fp[rows, pl.ds(n, T)].T
        embed(rows, count)
        diagonal(first, count)
        cross(pl.ds(0, half), rows)
        if p:
            cross(pl.ds(half, first - half), rows)

    demb[...] = (summed[...] * scale).astype(BF16)
    quarter = pl.ds(pl.multiple_of(blk * T, T), T)
    for r in range(0, rows_all, 2 * T):
        rows = pl.ds(r, 2 * T)
        back = dot_nt(demb[rows, :], w2[quarter, :])
        dpre[rows, :] = (back * gate[rows, quarter]).astype(BF16)

    x_copies, y_copies = [], []
    span = NZ // 2
    own = gy.shape[3]
    for i in range(2):
        rows = pl.ds(i * d_in // 2, d_in // 2)
        part = dot_nn(fpt[rows, :], dpre[...]).astype(BF16)
        for k in range(span):
            zz = i * span + k
            for xx in range(NX):
                for ll in range(2):
                    line = ((k * NX + xx) * 2 + ll) * own
                    gx[xx, zz, ll * own : (ll + 1) * own, :] = part[line : line + own, :128]
                    gy[ll, zz, xx] = part[line : line + own, 128:]
        zz = pl.ds(i * span, span)
        copy = remote(gy.at[1 - side, zz], ry.at[zz], ys.at[i], yr.at[i], pair)
        y_copies.append(copy)
        copy.start()
        for k in (2, 1, 3):
            copy = remote(
                gx.at[(x + k) % NX, zz], rx.at[k - 1, zz],
                xs.at[i, k - 1], xr.at[i, k - 1], x_peers[k - 1],
            )
            x_copies.append(copy)
            copy.start()

    cols = width // 4
    part = dot_nn(hidt[...], demb[:, pl.ds(pl.multiple_of(blk * cols, cols), cols)])
    gz[...] = part.astype(BF16).reshape(gz.shape)
    z_copies = [
        remote(gz.at[(z + k) % NZ], rz.at[k - 1], zs.at[k - 1], zr.at[k - 1], z_peers[k - 1])
        for k in (4, 3, 5, 2, 6, 1, 7)
    ]
    for copy in z_copies:
        copy.start()

    def total(mine, others):
        out = mine.astype(F32)
        for k in range(others.shape[0]):
            out = out + others[k].astype(F32)
        return out

    more = []
    for i in range(2):
        y_copies[i].wait()
        zz = pl.ds(i * span, span)
        for xx in range(NX):
            hy[xx, zz] = (gy[side, zz, xx].astype(F32) + ry[zz, xx].astype(F32)).astype(BF16)
        for k in (2, 1, 3):
            copy = remote(
                hy.at[(x + k) % NX, zz], qy.at[k - 1, zz],
                ys2.at[i, k - 1], yr2.at[i, k - 1], x_peers[k - 1],
            )
            more.append(copy)
            copy.start()
    y_copies = more

    for copy in x_copies:
        copy.wait()
    hx[...] = total(gx[x], rx).astype(BF16)
    x_copies = [
        remote(hx.at[(z + k) % NZ], qx.at[k - 1], xs2.at[k - 1], xr2.at[k - 1], z_peers[k - 1])
        for k in (4, 3, 5, 2, 6, 1, 7)
    ]
    for copy in x_copies:
        copy.start()

    for copy in z_copies:
        copy.wait()
    hz[...] = total(gz[z], rz).reshape(hz.shape)
    z_copies = [
        remote(hz.at[(x + k) % NX], qz.at[k - 1], zs2.at[k - 1], zr2.at[k - 1], x_peers[k - 1])
        for k in (2, 1, 3)
    ]
    for copy in z_copies:
        copy.start()

    for copy in y_copies:
        copy.wait()
    ky[...] = total(hy[x], qy)
    copies = [
        remote(ky.at[(z + k) % NZ], qky.at[k - 1], s3.at[k - 1], t3.at[k - 1], z_peers[k - 1])
        for k in (4, 3, 5, 2, 6, 1, 7)
    ]
    for copy in copies:
        copy.start()

    for copy in z_copies:
        copy.wait()
    kz[...] = total(hz[x], qz).reshape(kz.shape)
    z_copy = remote(kz.at[1 - side], r3z, zs3, zr3, pair)
    z_copy.start()
    for copy in x_copies:
        copy.wait()
    kx[...] = total(hx[z], qx).reshape(kx.shape)
    x_copy = remote(kx.at[1 - side], r3x, xs3, xr3, pair)
    x_copy.start()
    z_copy.wait()
    f2[...] = kz[side] + r3z[...]

    def spread(src, dst, i):
        out = [
            remote(src, dst.at[blk], s4.at[i, k], t4.at[i, k], peer)
            for k, peer in enumerate((cross_far, far, near))
        ]
        for copy in out:
            copy.start()
        return out

    last = spread(f2, r2, 0)
    x_copy.wait()
    f1[0] = kx[side] + r3x[...]
    last += spread(f1.at[0], r1.at[0], 1)
    for copy in copies:
        copy.wait()
    f1[1] = total(ky[z], qky)
    last += spread(f1.at[1], r1.at[1], 2)
    for i in range(2):
        r1[i, blk] = f1[i]
    r2[blk] = f2[...]
    for copy in last:
        copy.wait()
    for q in range(4):
        for i in range(2):
            o1[:, (2 * q + i) * 128 : (2 * q + i + 1) * 128] = r1[i, q]
        o2[:, q * o2.shape[1] // 4 : (q + 1) * o2.shape[1] // 4] = r2[q]


def gradients(fingerprints, w_first, w_second, scale):
    tok, d_in = fingerprints.shape
    hidden, width = w_second.shape
    rows = 4 * tok
    pieces = len(SPLIT)
    hbm_spec = pl.BlockSpec(memory_space=pltpu.HBM)
    vmem_spec = pl.BlockSpec(memory_space=pltpu.VMEM)
    c1, c2 = hidden // 4, width // 4
    n1, n2 = d_in // (NZ * NX * 2), hidden // (NZ * NX * 2)
    dma = pltpu.SemaphoreType.DMA
    return pl.pallas_call(
        functools.partial(step_kernel, scale),
        out_shape=(
            jax.ShapeDtypeStruct((n1, 4 * c1), F32),
            jax.ShapeDtypeStruct((n2, 4 * c2), F32),
        ),
        in_specs=[hbm_spec] * 3,
        out_specs=(vmem_spec, vmem_spec),
        scratch_shapes=[
            pltpu.VMEM((rows, d_in), BF16),
            pltpu.VMEM((d_in, rows), BF16),
            pltpu.VMEM((d_in, hidden), BF16),
            pltpu.VMEM((hidden, width), BF16),
            pltpu.VMEM((2 * tok, hidden), BF16),
            pltpu.VMEM((hidden, rows), BF16),
            pltpu.VMEM((rows, width), BF16),
            pltpu.VMEM((rows, width), F32),
            pltpu.VMEM((rows, hidden), F32),
            pltpu.VMEM((rows, width), BF16),
            pltpu.VMEM((rows, hidden // 4), BF16),
            pltpu.VMEM((rows, 128), F32),
            pltpu.VMEM((8, rows), F32),
            pltpu.VMEM((NX, NZ, 2 * n1, 128), BF16),
            pltpu.VMEM((NX - 1, NZ, 2 * n1, 128), BF16),
            pltpu.VMEM((2, NZ, NX, n1, 128), BF16),
            pltpu.VMEM((NZ, NX, n1, 128), BF16),
            pltpu.VMEM((NZ, NX * 2 * n2, c2), BF16),
            pltpu.VMEM((NZ - 1, NX * 2 * n2, c2), BF16),
            pltpu.VMEM((NZ, 2 * n1, 128), BF16),
            pltpu.VMEM((NZ - 1, 2 * n1, 128), BF16),
            pltpu.VMEM((NX, NZ, n1, 128), BF16),
            pltpu.VMEM((NX - 1, NZ, n1, 128), BF16),
            pltpu.VMEM((NX, 2 * n2, c2), F32),
            pltpu.VMEM((NX - 1, 2 * n2, c2), F32),
            pltpu.VMEM((2, n1, 128), F32),
            pltpu.VMEM((n1, 128), F32),
            pltpu.VMEM((NZ, n1, 128), F32),
            pltpu.VMEM((NZ - 1, n1, 128), F32),
            pltpu.VMEM((2, n2, c2), F32),
            pltpu.VMEM((n2, c2), F32),
            pltpu.VMEM((2, n1, 128), F32),
            pltpu.VMEM((2, 4, n1, 128), F32),
            pltpu.VMEM((n2, c2), F32),
            pltpu.VMEM((4, n2, c2), F32),
            dma((3,)),
            dma((pieces + 1,)),
            dma((pieces + 1,)),
            dma((pieces,)),
            dma((pieces,)),
            dma((2, NX - 1)),
            dma((2, NX - 1)),
            dma((2,)),
            dma((2,)),
            dma((NZ - 1,)),
            dma((NZ - 1,)),
            dma((NZ - 1,)),
            dma((NZ - 1,)),
            dma((2, NX - 1)),
            dma((2, NX - 1)),
            dma((NX - 1,)),
            dma((NX - 1,)),
            dma,
            dma,
            dma((NZ - 1,)),
            dma((NZ - 1,)),
            dma,
            dma,
            dma((3, 3)),
            dma((3, 3)),
        ],
        compiler_params=pltpu.CompilerParams(
            collective_id=0, has_side_effects=True, vmem_limit_bytes=55500000
        ),
        name="gradients",
    )(fingerprints, w_first, w_second)


def per_device(fingerprints, w_first, w_second):
    group_rows = fingerprints.shape[0] * lax.axis_size("blk")
    all_rows = group_rows * lax.axis_size("dp")
    scale = 2.0 / math.sqrt(group_rows * all_rows)
    return gradients(fingerprints, w_first, w_second, scale)


def solution(mesh):
    in_specs = (P(("blk", "dp"), None), P(), P())
    out_specs = (P("dp", None), P("dp", None))
    return jax.shard_map(
        per_device, mesh=mesh, in_specs=in_specs, out_specs=out_specs, check_vma=False
    )
```

```python
import functools
import math

import jax
import jax.numpy as jnp
from jax import lax
from jax.experimental import pallas as pl
from jax.experimental.pallas import tpu as pltpu
from jax.sharding import PartitionSpec as P

MESH = pl.DeviceIdType.MESH
F32 = jnp.float32
BF16 = jnp.bfloat16
NZ, NX = 8, 4
T = 256
PARTS = 4
SPLIT = (2, 2, 1, 1)


def dot_nt(a, b):
    return lax.dot_general(a, b, (((1,), (1,)), ((), ())), preferred_element_type=F32)


def dot_nn(a, b):
    return jnp.dot(a, b, preferred_element_type=F32)


def step_kernel(
    scale, fp_in, w1_in, w2_in, o1, o2,
    fp, fpt, w1, w2, hid, hidt, emb, summed, gate, demb, dpre, sqc, sqr,
    gx, rx, gy, ry, gz, rz, hx, qx, hy, qy, hz, qz, kx, r3x, ky, qky, kz, r3z, f1, r1, f2, r2,
    ready, load_sem, send_sem, recv_sem, pass_send, pass_recv,
    xs, xr, ys, yr, zs, zr, xs2, xr2, ys2, yr2, zs2, zr2, xs3, xr3, s3, t3, zs3, zr3, s4, t4,
):
    blk = lax.axis_index("blk")
    dp = lax.axis_index("dp")
    z, x = dp // 8, (dp // 2) % 4
    y, c = (blk // 2) * 2 + dp % 2, blk % 2
    tok, d_in = fp_in.shape
    hidden, width = w2_in.shape
    half = 2 * tok
    rows_all = 4 * tok
    pieces = len(SPLIT)
    sizes = [tok * share // sum(SPLIT) for share in SPLIT]
    firsts = [sum(sizes[:p]) for p in range(pieces)]
    norm = 1.0 / math.sqrt(width)

    def at(z, x, y, c):
        return {"blk": (y // 2) * 2 + c, "dp": (z * NX + x) * 2 + y % 2}

    side = y % 2
    far = at(z, x, (y + 2) % 4, c)
    near = at(z, x, y, 1 - c)
    cross_far = at(z, x, (y + 2) % 4, 1 - c)
    pair = at(z, x, (y // 2) * 2 + 1 - side, c)
    x_peers = [at(z, (x + k) % NX, y, c) for k in range(1, NX)]
    z_peers = [at((z + k) % NZ, x, y, c) for k in range(1, NZ)]
    steps = [z_peers[k % NZ - 1] for k in (2, -2)]
    peers = [far, near, cross_far, pair] + x_peers + steps + [z_peers[0], z_peers[NZ - 2]]

    barrier = pltpu.get_barrier_semaphore()
    for peer in peers:
        pl.semaphore_signal(barrier, inc=1, device_id=peer, device_id_type=MESH)
    loads = [
        pltpu.make_async_copy(fp_in, fp.at[pl.ds(0, tok)], load_sem.at[0]),
        pltpu.make_async_copy(w1_in, w1, load_sem.at[1]),
        pltpu.make_async_copy(w2_in, w2, load_sem.at[2]),
    ]
    loads[0].start()
    pl.semaphore_wait(barrier, len(peers))

    def remote(src, dst, send, recv, peer):
        return pltpu.make_async_remote_copy(
            src_ref=src, dst_ref=dst, send_sem=send, recv_sem=recv,
            device_id=peer, device_id_type=MESH,
        )

    def far_copy(p):
        return remote(
            fp_in.at[pl.ds(firsts[p], sizes[p])],
            fp.at[pl.ds(half + 2 * firsts[p], sizes[p])],
            send_sem.at[p], recv_sem.at[p], far,
        )

    def passing(p):
        return remote(
            fp.at[pl.ds(half + 2 * firsts[p], sizes[p])],
            fp.at[pl.ds(half + 2 * firsts[p] + sizes[p], sizes[p])],
            pass_send.at[p], pass_recv.at[p], near,
        )

    near_copy = remote(
        fp_in, fp.at[pl.ds(tok, tok)], send_sem.at[pieces], recv_sem.at[pieces], near
    )
    for p in range(pieces):
        far_copy(p).start()
    near_copy.start()
    for load in loads[1:]:
        load.start()
    for peer in steps:
        pl.semaphore_signal(ready, inc=1, device_id=peer, device_id_type=MESH)
    for load in loads:
        load.wait()
    near_copy.wait()

    def encode_columns(rows, cols):
        pre = dot_nn(fp[rows, :], w1[:, cols])
        sig = 1.0 / (1.0 + jnp.exp(-pre))
        h = (pre * sig).astype(BF16)
        hid[pl.ds(0, h.shape[0]), cols] = h
        hidt[cols, rows] = h.T
        gate[rows, cols] = sig * (1.0 + pre * (1.0 - sig))

    def embed(rows, count):
        emb[rows, :] = dot_nn(hid[pl.ds(0, count), :], w2[...]).astype(BF16)

    def residual(upper, lower):
        inter = dot_nt(fp[upper, :], fp[lower, :])
        den = sqc[upper, :][:, :1] + sqr[:1, lower] - inter
        pred = dot_nt(emb[upper, :], emb[lower, :])
        return (pred * norm - inter / den).astype(BF16)

    def diagonal(first, count):
        rows = pl.ds(first, count)
        inter = dot_nt(fp[rows, :], fp[rows, :])
        r_id = lax.broadcasted_iota(jnp.int32, (count, count), 0)
        c_id = lax.broadcasted_iota(jnp.int32, (count, count), 1)
        diag = jnp.where(r_id == c_id, inter, 0.0)
        col = jnp.sum(diag, axis=1, keepdims=True)
        row = jnp.sum(diag, axis=0, keepdims=True)
        sqc[rows, :] = jnp.broadcast_to(col, (count, 128))
        sqr[:, rows] = jnp.broadcast_to(row, (8, count))
        pred = dot_nt(emb[rows, :], emb[rows, :])
        resid = (pred * norm - inter / (col + row - inter)).astype(BF16)
        summed[rows, :] = dot_nn(resid, emb[rows, :])

    def cross(upper, lower):
        resid = residual(upper, lower)
        summed[upper, :] += dot_nn(resid, emb[lower, :])
        summed[lower, :] += dot_nn(resid.T, emb[upper, :])

    @pl.loop(0, hidden // T)
    def _(n):
        cols = pl.ds(pl.multiple_of(n * T, T), T)
        encode_columns(pl.ds(0, half), cols)

    @pl.loop(0, d_in // T)
    def _(n):
        cols = pl.ds(pl.multiple_of(n * T, T), T)
        fpt[cols, pl.ds(0, half)] = fp[pl.ds(0, half), cols].T

    embed(pl.ds(0, half), half)
    pl.semaphore_wait(ready, len(steps))
    for r in range(0, half, T):
        diagonal(r, T)
        if r:
            cross(pl.ds(0, r), pl.ds(r, T))

    for p in range(pieces):
        first, count = half + 2 * firsts[p], 2 * sizes[p]
        rows = pl.ds(first, count)
        far_copy(p).wait()
        passing(p).start()
        passing(p).wait()
        for n in range(0, hidden, T):
            encode_columns(rows, pl.ds(n, T))
        for n in range(0, d_in, T):
            fpt[pl.ds(n, T), rows] = fp[rows, pl.ds(n, T)].T
        embed(rows, count)
        diagonal(first, count)
        cross(pl.ds(0, half), rows)
        if p:
            cross(pl.ds(half, first - half), rows)

    demb[...] = (summed[...] * scale).astype(BF16)
    quarter = pl.ds(pl.multiple_of(blk * T, T), T)
    for r in range(0, rows_all, 2 * T):
        rows = pl.ds(r, 2 * T)
        back = dot_nt(demb[rows, :], w2[quarter, :])
        dpre[rows, :] = (back * gate[rows, quarter]).astype(BF16)

    x_copies, y_copies = [], []
    span = NZ // PARTS
    own = gy.shape[3]
    for i in range(PARTS):
        rows = pl.ds(i * d_in // PARTS, d_in // PARTS)
        part = dot_nn(fpt[rows, :], dpre[...]).astype(BF16)
        for k in range(span):
            zz = i * span + k
            for xx in range(NX):
                for ll in range(2):
                    line = ((k * NX + xx) * 2 + ll) * own
                    gx[xx, zz, ll * own : (ll + 1) * own, :] = part[line : line + own, :128]
                    gy[ll, zz, xx] = part[line : line + own, 128:]
        zz = pl.ds(i * span, span)
        copy = remote(gy.at[1 - side, zz], ry.at[zz], ys.at[i], yr.at[i], pair)
        y_copies.append(copy)
        copy.start()
        for k in (2, 1, 3):
            copy = remote(
                gx.at[(x + k) % NX, zz], rx.at[k - 1, zz],
                xs.at[i, k - 1], xr.at[i, k - 1], x_peers[k - 1],
            )
            x_copies.append(copy)
            copy.start()

    cols = width // 4
    part = dot_nn(hidt[...], demb[:, pl.ds(pl.multiple_of(blk * cols, cols), cols)])
    gz[...] = part.astype(BF16).reshape(gz.shape)
    z_copies = [
        remote(gz.at[(z + k) % NZ], rz.at[k - 1], zs.at[k - 1], zr.at[k - 1], z_peers[k - 1])
        for k in (4, 3, 5, 2, 6, 1, 7)
    ]
    for copy in z_copies:
        copy.start()

    def total(mine, others):
        out = mine.astype(F32)
        for k in range(others.shape[0]):
            out = out + others[k].astype(F32)
        return out

    more = []
    for i in range(PARTS):
        y_copies[i].wait()
        zz = pl.ds(i * span, span)
        for xx in range(NX):
            hy[xx, zz] = (gy[side, zz, xx].astype(F32) + ry[zz, xx].astype(F32)).astype(BF16)
        for k in (2, 1, 3):
            copy = remote(
                hy.at[(x + k) % NX, zz], qy.at[k - 1, zz],
                ys2.at[i, k - 1], yr2.at[i, k - 1], x_peers[k - 1],
            )
            more.append(copy)
            copy.start()
    y_copies = more

    for copy in x_copies:
        copy.wait()
    hx[...] = total(gx[x], rx).astype(BF16)
    x_copies = [
        remote(hx.at[(z + k) % NZ], qx.at[k - 1], xs2.at[k - 1], xr2.at[k - 1], z_peers[k - 1])
        for k in (4, 3, 5, 2, 6, 1, 7)
    ]
    for copy in x_copies:
        copy.start()

    def level(zz):
        return remote(
            ky.at[zz], qky.at[z], s3.at[zz], t3.at[z], at(zz, x, y, c)
        )

    def arrival(zz):
        return remote(
            ky.at[zz], qky.at[zz], s3.at[zz], t3.at[zz], at(zz, x, y, c)
        )

    for i in range(PARTS):
        for copy in y_copies[i * (NX - 1) : (i + 1) * (NX - 1)]:
            copy.wait()
        for zz in range(i * span, (i + 1) * span):
            ky[zz] = total(hy[x, zz], qy[:, zz])

            @pl.when(z != zz)
            def _(zz=zz):
                level(zz).start()

    for copy in z_copies:
        copy.wait()
    hz[...] = total(gz[z], rz).reshape(hz.shape)
    z_copies = [
        remote(hz.at[(x + k) % NX], qz.at[k - 1], zs2.at[k - 1], zr2.at[k - 1], x_peers[k - 1])
        for k in (2, 1, 3)
    ]
    for copy in z_copies:
        copy.start()

    for copy in z_copies:
        copy.wait()
    kz[...] = total(hz[x], qz).reshape(kz.shape)
    z_copy = remote(kz.at[1 - side], r3z, zs3, zr3, pair)
    z_copy.start()
    for copy in x_copies:
        copy.wait()
    kx[...] = total(hx[z], qx).reshape(kx.shape)
    x_copy = remote(kx.at[1 - side], r3x, xs3, xr3, pair)
    x_copy.start()
    z_copy.wait()
    f2[...] = kz[side] + r3z[...]

    def spread(src, dst, i):
        out = [
            remote(src, dst.at[blk], s4.at[i, k], t4.at[i, k], peer)
            for k, peer in enumerate((cross_far, far, near))
        ]
        for copy in out:
            copy.start()
        return out

    last = spread(f2, r2, 0)
    x_copy.wait()
    f1[0] = kx[side] + r3x[...]
    last += spread(f1.at[0], r1.at[0], 1)
    qky[z] = ky[z]
    for zz in range(NZ):

        @pl.when(z != zz)
        def _(zz=zz):
            arrival(zz).wait()

    part = qky[0]
    for zz in range(1, NZ):
        part = part + qky[zz]
    f1[1] = part
    last += spread(f1.at[1], r1.at[1], 2)
    for i in range(2):
        r1[i, blk] = f1[i]
    r2[blk] = f2[...]
    for copy in last:
        copy.wait()
    for q in range(4):
        for i in range(2):
            o1[:, (2 * q + i) * 128 : (2 * q + i + 1) * 128] = r1[i, q]
        o2[:, q * o2.shape[1] // 4 : (q + 1) * o2.shape[1] // 4] = r2[q]


def gradients(fingerprints, w_first, w_second, scale):
    tok, d_in = fingerprints.shape
    hidden, width = w_second.shape
    rows = 4 * tok
    pieces = len(SPLIT)
    hbm_spec = pl.BlockSpec(memory_space=pltpu.HBM)
    vmem_spec = pl.BlockSpec(memory_space=pltpu.VMEM)
    c1, c2 = hidden // 4, width // 4
    n1, n2 = d_in // (NZ * NX * 2), hidden // (NZ * NX * 2)
    dma = pltpu.SemaphoreType.DMA
    return pl.pallas_call(
        functools.partial(step_kernel, scale),
        out_shape=(
            jax.ShapeDtypeStruct((n1, 4 * c1), F32),
            jax.ShapeDtypeStruct((n2, 4 * c2), F32),
        ),
        in_specs=[hbm_spec] * 3,
        out_specs=(vmem_spec, vmem_spec),
        scratch_shapes=[
            pltpu.VMEM((rows, d_in), BF16),
            pltpu.VMEM((d_in, rows), BF16),
            pltpu.VMEM((d_in, hidden), BF16),
            pltpu.VMEM((hidden, width), BF16),
            pltpu.VMEM((2 * tok, hidden), BF16),
            pltpu.VMEM((hidden, rows), BF16),
            pltpu.VMEM((rows, width), BF16),
            pltpu.VMEM((rows, width), F32),
            pltpu.VMEM((rows, hidden), F32),
            pltpu.VMEM((rows, width), BF16),
            pltpu.VMEM((rows, hidden // 4), BF16),
            pltpu.VMEM((rows, 128), F32),
            pltpu.VMEM((8, rows), F32),
            pltpu.VMEM((NX, NZ, 2 * n1, 128), BF16),
            pltpu.VMEM((NX - 1, NZ, 2 * n1, 128), BF16),
            pltpu.VMEM((2, NZ, NX, n1, 128), BF16),
            pltpu.VMEM((NZ, NX, n1, 128), BF16),
            pltpu.VMEM((NZ, NX * 2 * n2, c2), BF16),
            pltpu.VMEM((NZ - 1, NX * 2 * n2, c2), BF16),
            pltpu.VMEM((NZ, 2 * n1, 128), BF16),
            pltpu.VMEM((NZ - 1, 2 * n1, 128), BF16),
            pltpu.VMEM((NX, NZ, n1, 128), BF16),
            pltpu.VMEM((NX - 1, NZ, n1, 128), BF16),
            pltpu.VMEM((NX, 2 * n2, c2), F32),
            pltpu.VMEM((NX - 1, 2 * n2, c2), F32),
            pltpu.VMEM((2, n1, 128), F32),
            pltpu.VMEM((n1, 128), F32),
            pltpu.VMEM((NZ, n1, 128), F32),
            pltpu.VMEM((NZ, n1, 128), F32),
            pltpu.VMEM((2, n2, c2), F32),
            pltpu.VMEM((n2, c2), F32),
            pltpu.VMEM((2, n1, 128), F32),
            pltpu.VMEM((2, 4, n1, 128), F32),
            pltpu.VMEM((n2, c2), F32),
            pltpu.VMEM((4, n2, c2), F32),
            pltpu.SemaphoreType.REGULAR,
            dma((3,)),
            dma((pieces + 1,)),
            dma((pieces + 1,)),
            dma((pieces,)),
            dma((pieces,)),
            dma((PARTS, NX - 1)),
            dma((PARTS, NX - 1)),
            dma((PARTS,)),
            dma((PARTS,)),
            dma((NZ - 1,)),
            dma((NZ - 1,)),
            dma((NZ - 1,)),
            dma((NZ - 1,)),
            dma((PARTS, NX - 1)),
            dma((PARTS, NX - 1)),
            dma((NX - 1,)),
            dma((NX - 1,)),
            dma,
            dma,
            dma((NZ,)),
            dma((NZ,)),
            dma,
            dma,
            dma((3, 3)),
            dma((3, 3)),
        ],
        compiler_params=pltpu.CompilerParams(
            collective_id=0, has_side_effects=True, vmem_limit_bytes=55500000
        ),
        name="gradients",
    )(fingerprints, w_first, w_second)


def per_device(fingerprints, w_first, w_second):
    group_rows = fingerprints.shape[0] * lax.axis_size("blk")
    all_rows = group_rows * lax.axis_size("dp")
    scale = 2.0 / math.sqrt(group_rows * all_rows)
    return gradients(fingerprints, w_first, w_second, scale)


def solution(mesh):
    in_specs = (P(("blk", "dp"), None), P(), P())
    out_specs = (P("dp", None), P("dp", None))
    return jax.shard_map(
        per_device, mesh=mesh, in_specs=in_specs, out_specs=out_specs, check_vma=False
    )
```

```python
import functools
import math

import jax
import jax.numpy as jnp
from jax import lax
from jax.experimental import pallas as pl
from jax.experimental.pallas import tpu as pltpu
from jax.sharding import PartitionSpec as P

MESH = pl.DeviceIdType.MESH
F32 = jnp.float32
BF16 = jnp.bfloat16
NZ, NX = 8, 4
T = 256
PARTS = 2
SPLIT = (3, 2, 1)


def dot_nt(a, b):
    return lax.dot_general(a, b, (((1,), (1,)), ((), ())), preferred_element_type=F32)


def dot_nn(a, b):
    return jnp.dot(a, b, preferred_element_type=F32)


def step_kernel(
    scale, fp_in, w1_in, w2_in, o1, o2,
    fp, fpt, w1, w2, hid, hidt, emb, summed, gate, demb, dpre, sqc, sqr,
    gx, rx, gy, ry, gz, rz, hx, qx, hy, qy, hz, qz, kx, r3x, ky, qky, kz, r3z, f1, r1, f2, r2,
    ready, load_sem, send_sem, recv_sem, pass_send, pass_recv,
    xs, xr, ys, yr, zs, zr, xs2, xr2, ys2, yr2, zs2, zr2, xs3, xr3, s3, t3, zs3, zr3, s4, t4,
):
    blk = lax.axis_index("blk")
    dp = lax.axis_index("dp")
    z, x = dp // 8, (dp // 2) % 4
    y, c = (blk // 2) * 2 + dp % 2, blk % 2
    tok, d_in = fp_in.shape
    hidden, width = w2_in.shape
    half = 2 * tok
    rows_all = 4 * tok
    pieces = len(SPLIT)
    sizes = [tok * share // sum(SPLIT) for share in SPLIT]
    firsts = [sum(sizes[:p]) for p in range(pieces)]
    norm = 1.0 / math.sqrt(width)

    def at(z, x, y, c):
        return {"blk": (y // 2) * 2 + c, "dp": (z * NX + x) * 2 + y % 2}

    side = y % 2
    far = at(z, x, (y + 2) % 4, c)
    near = at(z, x, y, 1 - c)
    cross_far = at(z, x, (y + 2) % 4, 1 - c)
    pair = at(z, x, (y // 2) * 2 + 1 - side, c)
    x_peers = [at(z, (x + k) % NX, y, c) for k in range(1, NX)]
    z_peers = [at((z + k) % NZ, x, y, c) for k in range(1, NZ)]
    steps = [z_peers[k % NZ - 1] for k in (2, -2)]
    peers = [far, near, cross_far, pair] + x_peers + steps + [z_peers[0], z_peers[NZ - 2]]

    barrier = pltpu.get_barrier_semaphore()
    for peer in peers:
        pl.semaphore_signal(barrier, inc=1, device_id=peer, device_id_type=MESH)
    loads = [
        pltpu.make_async_copy(fp_in, fp.at[pl.ds(0, tok)], load_sem.at[0]),
        pltpu.make_async_copy(w1_in, w1, load_sem.at[1]),
        pltpu.make_async_copy(w2_in, w2, load_sem.at[2]),
    ]
    loads[0].start()
    pl.semaphore_wait(barrier, len(peers))

    def remote(src, dst, send, recv, peer):
        return pltpu.make_async_remote_copy(
            src_ref=src, dst_ref=dst, send_sem=send, recv_sem=recv,
            device_id=peer, device_id_type=MESH,
        )

    def far_copy(p):
        return remote(
            fp_in.at[pl.ds(firsts[p], sizes[p])],
            fp.at[pl.ds(half + 2 * firsts[p], sizes[p])],
            send_sem.at[p], recv_sem.at[p], far,
        )

    def passing(p):
        return remote(
            fp.at[pl.ds(half + 2 * firsts[p], sizes[p])],
            fp.at[pl.ds(half + 2 * firsts[p] + sizes[p], sizes[p])],
            pass_send.at[p], pass_recv.at[p], near,
        )

    near_copy = remote(
        fp_in, fp.at[pl.ds(tok, tok)], send_sem.at[pieces], recv_sem.at[pieces], near
    )
    for p in range(pieces):
        far_copy(p).start()
    near_copy.start()
    for load in loads[1:]:
        load.start()
    for peer in steps:
        pl.semaphore_signal(ready, inc=1, device_id=peer, device_id_type=MESH)
    for load in loads:
        load.wait()
    near_copy.wait()

    def encode_columns(rows, cols):
        pre = dot_nn(fp[rows, :], w1[:, cols])
        sig = 1.0 / (1.0 + jnp.exp(-pre))
        h = (pre * sig).astype(BF16)
        hid[pl.ds(0, h.shape[0]), cols] = h
        hidt[cols, rows] = h.T
        gate[rows, cols] = sig * (1.0 + pre * (1.0 - sig))

    def embed(rows, count):
        emb[rows, :] = dot_nn(hid[pl.ds(0, count), :], w2[...]).astype(BF16)

    def residual(upper, lower):
        inter = dot_nt(fp[upper, :], fp[lower, :])
        den = sqc[upper, :][:, :1] + sqr[:1, lower] - inter
        pred = dot_nt(emb[upper, :], emb[lower, :])
        return (pred * norm - inter / den).astype(BF16)

    def diagonal(first, count):
        rows = pl.ds(first, count)
        inter = dot_nt(fp[rows, :], fp[rows, :])
        r_id = lax.broadcasted_iota(jnp.int32, (count, count), 0)
        c_id = lax.broadcasted_iota(jnp.int32, (count, count), 1)
        diag = jnp.where(r_id == c_id, inter, 0.0)
        col = jnp.sum(diag, axis=1, keepdims=True)
        row = jnp.sum(diag, axis=0, keepdims=True)
        sqc[rows, :] = jnp.broadcast_to(col, (count, 128))
        sqr[:, rows] = jnp.broadcast_to(row, (8, count))
        pred = dot_nt(emb[rows, :], emb[rows, :])
        resid = (pred * norm - inter / (col + row - inter)).astype(BF16)
        summed[rows, :] = dot_nn(resid, emb[rows, :])

    def cross(upper, lower):
        resid = residual(upper, lower)
        summed[upper, :] += dot_nn(resid, emb[lower, :])
        summed[lower, :] += dot_nn(resid.T, emb[upper, :])

    @pl.loop(0, hidden // T)
    def _(n):
        cols = pl.ds(pl.multiple_of(n * T, T), T)
        encode_columns(pl.ds(0, half), cols)

    @pl.loop(0, d_in // T)
    def _(n):
        cols = pl.ds(pl.multiple_of(n * T, T), T)
        fpt[cols, pl.ds(0, half)] = fp[pl.ds(0, half), cols].T

    embed(pl.ds(0, half), half)
    pl.semaphore_wait(ready, len(steps))
    for r in range(0, half, T):
        diagonal(r, T)
        if r:
            cross(pl.ds(0, r), pl.ds(r, T))

    for p in range(pieces):
        first, count = half + 2 * firsts[p], 2 * sizes[p]
        rows = pl.ds(first, count)
        far_copy(p).wait()
        passing(p).start()
        passing(p).wait()
        for n in range(0, hidden, T):
            encode_columns(rows, pl.ds(n, T))
        for n in range(0, d_in, T):
            fpt[pl.ds(n, T), rows] = fp[rows, pl.ds(n, T)].T
        embed(rows, count)
        diagonal(first, count)
        cross(pl.ds(0, half), rows)
        if p:
            cross(pl.ds(half, first - half), rows)

    demb[...] = (summed[...] * scale).astype(BF16)
    quarter = pl.ds(pl.multiple_of(blk * T, T), T)
    for r in range(0, rows_all, 2 * T):
        rows = pl.ds(r, 2 * T)
        back = dot_nt(demb[rows, :], w2[quarter, :])
        dpre[rows, :] = (back * gate[rows, quarter]).astype(BF16)

    x_copies, y_copies = [], []
    span = NZ // PARTS
    own = gy.shape[3]
    for i in range(PARTS):
        rows = pl.ds(i * d_in // PARTS, d_in // PARTS)
        part = dot_nn(fpt[rows, :], dpre[...]).astype(BF16)
        for k in range(span):
            zz = i * span + k
            for xx in range(NX):
                for ll in range(2):
                    line = ((k * NX + xx) * 2 + ll) * own
                    gx[xx, zz, ll * own : (ll + 1) * own, :] = part[line : line + own, :128]
                    gy[ll, zz, xx] = part[line : line + own, 128:]
        zz = pl.ds(i * span, span)
        copy = remote(gy.at[1 - side, zz], ry.at[zz], ys.at[i], yr.at[i], pair)
        y_copies.append(copy)
        copy.start()
        for k in (2, 1, 3):
            copy = remote(
                gx.at[(x + k) % NX, zz], rx.at[k - 1, zz],
                xs.at[i, k - 1], xr.at[i, k - 1], x_peers[k - 1],
            )
            x_copies.append(copy)
            copy.start()

    cols = width // 4
    part = dot_nn(hidt[...], demb[:, pl.ds(pl.multiple_of(blk * cols, cols), cols)])
    gz[...] = part.astype(BF16).reshape(gz.shape)
    z_copies = [
        remote(gz.at[(z + k) % NZ], rz.at[k - 1], zs.at[k - 1], zr.at[k - 1], z_peers[k - 1])
        for k in (4, 3, 5, 2, 6, 1, 7)
    ]
    for copy in z_copies:
        copy.start()

    def total(mine, others):
        out = mine.astype(F32)
        for k in range(others.shape[0]):
            out = out + others[k].astype(F32)
        return out

    more = []
    for i in range(PARTS):
        y_copies[i].wait()
        zz = pl.ds(i * span, span)
        for xx in range(NX):
            hy[xx, zz] = (gy[side, zz, xx].astype(F32) + ry[zz, xx].astype(F32)).astype(BF16)
        for k in (2, 1, 3):
            copy = remote(
                hy.at[(x + k) % NX, zz], qy.at[k - 1, zz],
                ys2.at[i, k - 1], yr2.at[i, k - 1], x_peers[k - 1],
            )
            more.append(copy)
            copy.start()
    y_copies = more

    for copy in x_copies:
        copy.wait()
    hx[...] = total(gx[x], rx).astype(BF16)
    x_copies = [
        remote(hx.at[(z + k) % NZ], qx.at[k - 1], xs2.at[k - 1], xr2.at[k - 1], z_peers[k - 1])
        for k in (4, 3, 5, 2, 6, 1, 7)
    ]
    for copy in x_copies:
        copy.start()

    def level(zz):
        return remote(
            ky.at[zz], qky.at[z], s3.at[zz], t3.at[z], at(zz, x, y, c)
        )

    def arrival(zz):
        return remote(
            ky.at[zz], qky.at[zz], s3.at[zz], t3.at[zz], at(zz, x, y, c)
        )

    for i in range(PARTS):
        for copy in y_copies[i * (NX - 1) : (i + 1) * (NX - 1)]:
            copy.wait()
        for zz in range(i * span, (i + 1) * span):
            ky[zz] = total(hy[x, zz], qy[:, zz])

            @pl.when(z != zz)
            def _(zz=zz):
                level(zz).start()

    for copy in z_copies:
        copy.wait()
    hz[...] = total(gz[z], rz).reshape(hz.shape)
    z_copies = [
        remote(hz.at[(x + k) % NX], qz.at[k - 1], zs2.at[k - 1], zr2.at[k - 1], x_peers[k - 1])
        for k in (2, 1, 3)
    ]
    for copy in z_copies:
        copy.start()

    for copy in z_copies:
        copy.wait()
    kz[...] = total(hz[x], qz).reshape(kz.shape)
    z_copy = remote(kz.at[1 - side], r3z, zs3, zr3, pair)
    z_copy.start()
    for copy in x_copies:
        copy.wait()
    kx[...] = total(hx[z], qx).reshape(kx.shape)
    x_copy = remote(kx.at[1 - side], r3x, xs3, xr3, pair)
    x_copy.start()
    z_copy.wait()
    f2[...] = kz[side] + r3z[...]

    def spread(src, dst, i):
        out = [
            remote(src, dst.at[blk], s4.at[i, k], t4.at[i, k], peer)
            for k, peer in enumerate((cross_far, far, near))
        ]
        for copy in out:
            copy.start()
        return out

    last = spread(f2, r2, 0)
    x_copy.wait()
    f1[0] = kx[side] + r3x[...]
    last += spread(f1.at[0], r1.at[0], 1)
    qky[z] = ky[z]
    for zz in range(NZ):

        @pl.when(z != zz)
        def _(zz=zz):
            arrival(zz).wait()

    part = qky[0]
    for zz in range(1, NZ):
        part = part + qky[zz]
    f1[1] = part
    last += spread(f1.at[1], r1.at[1], 2)
    for i in range(2):
        r1[i, blk] = f1[i]
    r2[blk] = f2[...]
    for copy in last:
        copy.wait()
    for q in range(4):
        for i in range(2):
            o1[:, (2 * q + i) * 128 : (2 * q + i + 1) * 128] = r1[i, q]
        o2[:, q * o2.shape[1] // 4 : (q + 1) * o2.shape[1] // 4] = r2[q]


def gradients(fingerprints, w_first, w_second, scale):
    tok, d_in = fingerprints.shape
    hidden, width = w_second.shape
    rows = 4 * tok
    pieces = len(SPLIT)
    hbm_spec = pl.BlockSpec(memory_space=pltpu.HBM)
    vmem_spec = pl.BlockSpec(memory_space=pltpu.VMEM)
    c1, c2 = hidden // 4, width // 4
    n1, n2 = d_in // (NZ * NX * 2), hidden // (NZ * NX * 2)
    dma = pltpu.SemaphoreType.DMA
    return pl.pallas_call(
        functools.partial(step_kernel, scale),
        out_shape=(
            jax.ShapeDtypeStruct((n1, 4 * c1), F32),
            jax.ShapeDtypeStruct((n2, 4 * c2), F32),
        ),
        in_specs=[hbm_spec] * 3,
        out_specs=(vmem_spec, vmem_spec),
        scratch_shapes=[
            pltpu.VMEM((rows, d_in), BF16),
            pltpu.VMEM((d_in, rows), BF16),
            pltpu.VMEM((d_in, hidden), BF16),
            pltpu.VMEM((hidden, width), BF16),
            pltpu.VMEM((2 * tok, hidden), BF16),
            pltpu.VMEM((hidden, rows), BF16),
            pltpu.VMEM((rows, width), BF16),
            pltpu.VMEM((rows, width), F32),
            pltpu.VMEM((rows, hidden), F32),
            pltpu.VMEM((rows, width), BF16),
            pltpu.VMEM((rows, hidden // 4), BF16),
            pltpu.VMEM((rows, 128), F32),
            pltpu.VMEM((8, rows), F32),
            pltpu.VMEM((NX, NZ, 2 * n1, 128), BF16),
            pltpu.VMEM((NX - 1, NZ, 2 * n1, 128), BF16),
            pltpu.VMEM((2, NZ, NX, n1, 128), BF16),
            pltpu.VMEM((NZ, NX, n1, 128), BF16),
            pltpu.VMEM((NZ, NX * 2 * n2, c2), BF16),
            pltpu.VMEM((NZ - 1, NX * 2 * n2, c2), BF16),
            pltpu.VMEM((NZ, 2 * n1, 128), BF16),
            pltpu.VMEM((NZ - 1, 2 * n1, 128), BF16),
            pltpu.VMEM((NX, NZ, n1, 128), BF16),
            pltpu.VMEM((NX - 1, NZ, n1, 128), BF16),
            pltpu.VMEM((NX, 2 * n2, c2), F32),
            pltpu.VMEM((NX - 1, 2 * n2, c2), F32),
            pltpu.VMEM((2, n1, 128), F32),
            pltpu.VMEM((n1, 128), F32),
            pltpu.VMEM((NZ, n1, 128), F32),
            pltpu.VMEM((NZ, n1, 128), F32),
            pltpu.VMEM((2, n2, c2), F32),
            pltpu.VMEM((n2, c2), F32),
            pltpu.VMEM((2, n1, 128), F32),
            pltpu.VMEM((2, 4, n1, 128), F32),
            pltpu.VMEM((n2, c2), F32),
            pltpu.VMEM((4, n2, c2), F32),
            pltpu.SemaphoreType.REGULAR,
            dma((3,)),
            dma((pieces + 1,)),
            dma((pieces + 1,)),
            dma((pieces,)),
            dma((pieces,)),
            dma((PARTS, NX - 1)),
            dma((PARTS, NX - 1)),
            dma((PARTS,)),
            dma((PARTS,)),
            dma((NZ - 1,)),
            dma((NZ - 1,)),
            dma((NZ - 1,)),
            dma((NZ - 1,)),
            dma((PARTS, NX - 1)),
            dma((PARTS, NX - 1)),
            dma((NX - 1,)),
            dma((NX - 1,)),
            dma,
            dma,
            dma((NZ,)),
            dma((NZ,)),
            dma,
            dma,
            dma((3, 3)),
            dma((3, 3)),
        ],
        compiler_params=pltpu.CompilerParams(
            collective_id=0, has_side_effects=True, vmem_limit_bytes=55500000
        ),
        name="gradients",
    )(fingerprints, w_first, w_second)


def per_device(fingerprints, w_first, w_second):
    group_rows = fingerprints.shape[0] * lax.axis_size("blk")
    all_rows = group_rows * lax.axis_size("dp")
    scale = 2.0 / math.sqrt(group_rows * all_rows)
    return gradients(fingerprints, w_first, w_second, scale)


def solution(mesh):
    in_specs = (P(("blk", "dp"), None), P(), P())
    out_specs = (P("dp", None), P("dp", None))
    return jax.shard_map(
        per_device, mesh=mesh, in_specs=in_specs, out_specs=out_specs, check_vma=False
    )
```

```python
import functools
import math

import jax
import jax.numpy as jnp
from jax import lax
from jax.experimental import pallas as pl
from jax.experimental.pallas import tpu as pltpu
from jax.sharding import PartitionSpec as P

MESH = pl.DeviceIdType.MESH
F32 = jnp.float32
BF16 = jnp.bfloat16
NZ, NX = 8, 4
T = 256
PARTS = 2
SPLIT = (3, 2, 1)


def dot_nt(a, b):
    return lax.dot_general(a, b, (((1,), (1,)), ((), ())), preferred_element_type=F32)


def dot_nn(a, b):
    return jnp.dot(a, b, preferred_element_type=F32)


def step_kernel(
    scale, fp_in, w1_in, w2_in, o1, o2,
    fp, fpt, w1, w2, hid, hidt, emb, summed, gate, demb, dpre, sqc, sqr,
    gx, rx, gy, ry, gz, rz, hx, qx, hy, qy, hz, qz, kx, r3x, ky, qky, kz, r3z, f1, r1, f2, r2,
    ready, load_sem, send_sem, recv_sem, pass_send, pass_recv,
    xs, xr, ys, yr, zs, zr, xs2, xr2, ys2, yr2, zs2, zr2, xs3, xr3, s3, t3, zs3, zr3, s4, t4,
):
    blk = lax.axis_index("blk")
    dp = lax.axis_index("dp")
    z, x = dp // 8, (dp // 2) % 4
    y, c = (blk // 2) * 2 + dp % 2, blk % 2
    tok, d_in = fp_in.shape
    hidden, width = w2_in.shape
    half = 2 * tok
    rows_all = 4 * tok
    pieces = len(SPLIT)
    sizes = [tok * share // sum(SPLIT) for share in SPLIT]
    firsts = [sum(sizes[:p]) for p in range(pieces)]
    norm = 1.0 / math.sqrt(width)

    def at(z, x, y, c):
        return {"blk": (y // 2) * 2 + c, "dp": (z * NX + x) * 2 + y % 2}

    side = y % 2
    far = at(z, x, (y + 2) % 4, c)
    near = at(z, x, y, 1 - c)
    cross_far = at(z, x, (y + 2) % 4, 1 - c)
    pair = at(z, x, (y // 2) * 2 + 1 - side, c)
    x_peers = [at(z, (x + k) % NX, y, c) for k in range(1, NX)]
    z_peers = [at((z + k) % NZ, x, y, c) for k in range(1, NZ)]
    steps = [z_peers[k % NZ - 1] for k in (2, -2)]
    peers = [far, near, cross_far, pair] + x_peers + steps + [z_peers[0], z_peers[NZ - 2]]

    barrier = pltpu.get_barrier_semaphore()
    for peer in peers:
        pl.semaphore_signal(barrier, inc=1, device_id=peer, device_id_type=MESH)
    loads = [
        pltpu.make_async_copy(fp_in, fp.at[pl.ds(0, tok)], load_sem.at[0]),
        pltpu.make_async_copy(w1_in, w1, load_sem.at[1]),
        pltpu.make_async_copy(w2_in, w2, load_sem.at[2]),
    ]
    loads[0].start()
    pl.semaphore_wait(barrier, len(peers))

    def remote(src, dst, send, recv, peer):
        return pltpu.make_async_remote_copy(
            src_ref=src, dst_ref=dst, send_sem=send, recv_sem=recv,
            device_id=peer, device_id_type=MESH,
        )

    pending = []

    def landed(copy):
        copy.wait_recv()
        pending.append(copy)

    def far_copy(p):
        return remote(
            fp_in.at[pl.ds(firsts[p], sizes[p])],
            fp.at[pl.ds(half + 2 * firsts[p], sizes[p])],
            send_sem.at[p], recv_sem.at[p], far,
        )

    def passing(p):
        return remote(
            fp.at[pl.ds(half + 2 * firsts[p], sizes[p])],
            fp.at[pl.ds(half + 2 * firsts[p] + sizes[p], sizes[p])],
            pass_send.at[p], pass_recv.at[p], near,
        )

    near_copy = remote(
        fp_in, fp.at[pl.ds(tok, tok)], send_sem.at[pieces], recv_sem.at[pieces], near
    )
    for p in range(pieces):
        far_copy(p).start()
    near_copy.start()
    for load in loads[1:]:
        load.start()
    for peer in steps:
        pl.semaphore_signal(ready, inc=1, device_id=peer, device_id_type=MESH)
    for load in loads:
        load.wait()
    landed(near_copy)

    def encode_columns(rows, cols):
        pre = dot_nn(fp[rows, :], w1[:, cols])
        sig = 1.0 / (1.0 + jnp.exp(-pre))
        h = (pre * sig).astype(BF16)
        hid[pl.ds(0, h.shape[0]), cols] = h
        hidt[cols, rows] = h.T
        gate[rows, cols] = sig * (1.0 + pre * (1.0 - sig))

    def embed(rows, count):
        emb[rows, :] = dot_nn(hid[pl.ds(0, count), :], w2[...]).astype(BF16)

    def residual(upper, lower):
        inter = dot_nt(fp[upper, :], fp[lower, :])
        den = sqc[upper, :][:, :1] + sqr[:1, lower] - inter
        pred = dot_nt(emb[upper, :], emb[lower, :])
        return (pred * norm - inter / den).astype(BF16)

    def diagonal(first, count):
        rows = pl.ds(first, count)
        inter = dot_nt(fp[rows, :], fp[rows, :])
        r_id = lax.broadcasted_iota(jnp.int32, (count, count), 0)
        c_id = lax.broadcasted_iota(jnp.int32, (count, count), 1)
        diag = jnp.where(r_id == c_id, inter, 0.0)
        col = jnp.sum(diag, axis=1, keepdims=True)
        row = jnp.sum(diag, axis=0, keepdims=True)
        sqc[rows, :] = jnp.broadcast_to(col, (count, 128))
        sqr[:, rows] = jnp.broadcast_to(row, (8, count))
        pred = dot_nt(emb[rows, :], emb[rows, :])
        resid = (pred * norm - inter / (col + row - inter)).astype(BF16)
        summed[rows, :] = dot_nn(resid, emb[rows, :])

    def cross(upper, lower):
        resid = residual(upper, lower)
        summed[upper, :] += dot_nn(resid, emb[lower, :])
        summed[lower, :] += dot_nn(resid.T, emb[upper, :])

    @pl.loop(0, hidden // T)
    def _(n):
        cols = pl.ds(pl.multiple_of(n * T, T), T)
        encode_columns(pl.ds(0, half), cols)

    @pl.loop(0, d_in // T)
    def _(n):
        cols = pl.ds(pl.multiple_of(n * T, T), T)
        fpt[cols, pl.ds(0, half)] = fp[pl.ds(0, half), cols].T

    embed(pl.ds(0, half), half)
    pl.semaphore_wait(ready, len(steps))
    for r in range(0, half, T):
        diagonal(r, T)
        if r:
            cross(pl.ds(0, r), pl.ds(r, T))

    for p in range(pieces):
        first, count = half + 2 * firsts[p], 2 * sizes[p]
        rows = pl.ds(first, count)
        landed(far_copy(p))
        passing(p).start()
        landed(passing(p))
        for n in range(0, hidden, T):
            encode_columns(rows, pl.ds(n, T))
        for n in range(0, d_in, T):
            fpt[pl.ds(n, T), rows] = fp[rows, pl.ds(n, T)].T
        embed(rows, count)
        diagonal(first, count)
        cross(pl.ds(0, half), rows)
        if p:
            cross(pl.ds(half, first - half), rows)

    demb[...] = (summed[...] * scale).astype(BF16)
    quarter = pl.ds(pl.multiple_of(blk * T, T), T)
    for r in range(0, rows_all, 2 * T):
        rows = pl.ds(r, 2 * T)
        back = dot_nt(demb[rows, :], w2[quarter, :])
        dpre[rows, :] = (back * gate[rows, quarter]).astype(BF16)

    x_copies, y_copies = [], []
    span = NZ // PARTS
    own = gy.shape[3]
    for i in range(PARTS):
        rows = pl.ds(i * d_in // PARTS, d_in // PARTS)
        part = dot_nn(fpt[rows, :], dpre[...]).astype(BF16)
        for k in range(span):
            zz = i * span + k
            for xx in range(NX):
                for ll in range(2):
                    line = ((k * NX + xx) * 2 + ll) * own
                    gx[xx, zz, ll * own : (ll + 1) * own, :] = part[line : line + own, :128]
                    gy[ll, zz, xx] = part[line : line + own, 128:]
        zz = pl.ds(i * span, span)
        copy = remote(gy.at[1 - side, zz], ry.at[zz], ys.at[i], yr.at[i], pair)
        y_copies.append(copy)
        copy.start()
        for k in (2, 1, 3):
            copy = remote(
                gx.at[(x + k) % NX, zz], rx.at[k - 1, zz],
                xs.at[i, k - 1], xr.at[i, k - 1], x_peers[k - 1],
            )
            x_copies.append(copy)
            copy.start()

    cols = width // 4
    part = dot_nn(hidt[...], demb[:, pl.ds(pl.multiple_of(blk * cols, cols), cols)])
    gz[...] = part.astype(BF16).reshape(gz.shape)
    z_copies = [
        remote(gz.at[(z + k) % NZ], rz.at[k - 1], zs.at[k - 1], zr.at[k - 1], z_peers[k - 1])
        for k in (4, 3, 5, 2, 6, 1, 7)
    ]
    for copy in z_copies:
        copy.start()

    def total(mine, others):
        out = mine.astype(F32)
        for k in range(others.shape[0]):
            out = out + others[k].astype(F32)
        return out

    more = []
    for i in range(PARTS):
        landed(y_copies[i])
        zz = pl.ds(i * span, span)
        for xx in range(NX):
            hy[xx, zz] = (gy[side, zz, xx].astype(F32) + ry[zz, xx].astype(F32)).astype(BF16)
        for k in (2, 1, 3):
            copy = remote(
                hy.at[(x + k) % NX, zz], qy.at[k - 1, zz],
                ys2.at[i, k - 1], yr2.at[i, k - 1], x_peers[k - 1],
            )
            more.append(copy)
            copy.start()
    y_copies = more

    for copy in x_copies:
        landed(copy)
    hx[...] = total(gx[x], rx).astype(BF16)
    x_copies = [
        remote(hx.at[(z + k) % NZ], qx.at[k - 1], xs2.at[k - 1], xr2.at[k - 1], z_peers[k - 1])
        for k in (4, 3, 5, 2, 6, 1, 7)
    ]
    for copy in x_copies:
        copy.start()

    def level(zz):
        return remote(
            ky.at[zz], qky.at[z], s3.at[zz], t3.at[z], at(zz, x, y, c)
        )

    def arrival(zz):
        return remote(
            ky.at[zz], qky.at[zz], s3.at[zz], t3.at[zz], at(zz, x, y, c)
        )

    for i in range(PARTS):
        for copy in y_copies[i * (NX - 1) : (i + 1) * (NX - 1)]:
            landed(copy)
        for zz in range(i * span, (i + 1) * span):
            ky[zz] = total(hy[x, zz], qy[:, zz])

            @pl.when(z != zz)
            def _(zz=zz):
                level(zz).start()

    for copy in z_copies:
        landed(copy)
    hz[...] = total(gz[z], rz).reshape(hz.shape)
    z_copies = [
        remote(hz.at[(x + k) % NX], qz.at[k - 1], zs2.at[k - 1], zr2.at[k - 1], x_peers[k - 1])
        for k in (2, 1, 3)
    ]
    for copy in z_copies:
        copy.start()

    for copy in z_copies:
        landed(copy)
    kz[...] = total(hz[x], qz).reshape(kz.shape)
    z_copy = remote(kz.at[1 - side], r3z, zs3, zr3, pair)
    z_copy.start()
    for copy in x_copies:
        landed(copy)
    kx[...] = total(hx[z], qx).reshape(kx.shape)
    x_copy = remote(kx.at[1 - side], r3x, xs3, xr3, pair)
    x_copy.start()
    landed(z_copy)
    f2[...] = kz[side] + r3z[...]

    def spread(src, dst, i):
        out = [
            remote(src, dst.at[blk], s4.at[i, k], t4.at[i, k], peer)
            for k, peer in enumerate((cross_far, far, near))
        ]
        for copy in out:
            copy.start()
        return out

    last = spread(f2, r2, 0)
    landed(x_copy)
    f1[0] = kx[side] + r3x[...]
    last += spread(f1.at[0], r1.at[0], 1)
    qky[z] = ky[z]
    for zz in range(NZ):

        @pl.when(z != zz)
        def _(zz=zz):
            arrival(zz).wait()

    part = qky[0]
    for zz in range(1, NZ):
        part = part + qky[zz]
    f1[1] = part
    last += spread(f1.at[1], r1.at[1], 2)
    for i in range(2):
        r1[i, blk] = f1[i]
    r2[blk] = f2[...]
    for copy in last:
        landed(copy)
    for copy in pending:
        copy.wait_send()
    for q in range(4):
        for i in range(2):
            o1[:, (2 * q + i) * 128 : (2 * q + i + 1) * 128] = r1[i, q]
        o2[:, q * o2.shape[1] // 4 : (q + 1) * o2.shape[1] // 4] = r2[q]


def gradients(fingerprints, w_first, w_second, scale):
    tok, d_in = fingerprints.shape
    hidden, width = w_second.shape
    rows = 4 * tok
    pieces = len(SPLIT)
    hbm_spec = pl.BlockSpec(memory_space=pltpu.HBM)
    vmem_spec = pl.BlockSpec(memory_space=pltpu.VMEM)
    c1, c2 = hidden // 4, width // 4
    n1, n2 = d_in // (NZ * NX * 2), hidden // (NZ * NX * 2)
    dma = pltpu.SemaphoreType.DMA
    return pl.pallas_call(
        functools.partial(step_kernel, scale),
        out_shape=(
            jax.ShapeDtypeStruct((n1, 4 * c1), F32),
            jax.ShapeDtypeStruct((n2, 4 * c2), F32),
        ),
        in_specs=[hbm_spec] * 3,
        out_specs=(vmem_spec, vmem_spec),
        scratch_shapes=[
            pltpu.VMEM((rows, d_in), BF16),
            pltpu.VMEM((d_in, rows), BF16),
            pltpu.VMEM((d_in, hidden), BF16),
            pltpu.VMEM((hidden, width), BF16),
            pltpu.VMEM((2 * tok, hidden), BF16),
            pltpu.VMEM((hidden, rows), BF16),
            pltpu.VMEM((rows, width), BF16),
            pltpu.VMEM((rows, width), F32),
            pltpu.VMEM((rows, hidden), F32),
            pltpu.VMEM((rows, width), BF16),
            pltpu.VMEM((rows, hidden // 4), BF16),
            pltpu.VMEM((rows, 128), F32),
            pltpu.VMEM((8, rows), F32),
            pltpu.VMEM((NX, NZ, 2 * n1, 128), BF16),
            pltpu.VMEM((NX - 1, NZ, 2 * n1, 128), BF16),
            pltpu.VMEM((2, NZ, NX, n1, 128), BF16),
            pltpu.VMEM((NZ, NX, n1, 128), BF16),
            pltpu.VMEM((NZ, NX * 2 * n2, c2), BF16),
            pltpu.VMEM((NZ - 1, NX * 2 * n2, c2), BF16),
            pltpu.VMEM((NZ, 2 * n1, 128), BF16),
            pltpu.VMEM((NZ - 1, 2 * n1, 128), BF16),
            pltpu.VMEM((NX, NZ, n1, 128), BF16),
            pltpu.VMEM((NX - 1, NZ, n1, 128), BF16),
            pltpu.VMEM((NX, 2 * n2, c2), F32),
            pltpu.VMEM((NX - 1, 2 * n2, c2), F32),
            pltpu.VMEM((2, n1, 128), F32),
            pltpu.VMEM((n1, 128), F32),
            pltpu.VMEM((NZ, n1, 128), F32),
            pltpu.VMEM((NZ, n1, 128), F32),
            pltpu.VMEM((2, n2, c2), F32),
            pltpu.VMEM((n2, c2), F32),
            pltpu.VMEM((2, n1, 128), F32),
            pltpu.VMEM((2, 4, n1, 128), F32),
            pltpu.VMEM((n2, c2), F32),
            pltpu.VMEM((4, n2, c2), F32),
            pltpu.SemaphoreType.REGULAR,
            dma((3,)),
            dma((pieces + 1,)),
            dma((pieces + 1,)),
            dma((pieces,)),
            dma((pieces,)),
            dma((PARTS, NX - 1)),
            dma((PARTS, NX - 1)),
            dma((PARTS,)),
            dma((PARTS,)),
            dma((NZ - 1,)),
            dma((NZ - 1,)),
            dma((NZ - 1,)),
            dma((NZ - 1,)),
            dma((PARTS, NX - 1)),
            dma((PARTS, NX - 1)),
            dma((NX - 1,)),
            dma((NX - 1,)),
            dma,
            dma,
            dma((NZ,)),
            dma((NZ,)),
            dma,
            dma,
            dma((3, 3)),
            dma((3, 3)),
        ],
        compiler_params=pltpu.CompilerParams(
            collective_id=0, has_side_effects=True, vmem_limit_bytes=55500000
        ),
        name="gradients",
    )(fingerprints, w_first, w_second)


def per_device(fingerprints, w_first, w_second):
    group_rows = fingerprints.shape[0] * lax.axis_size("blk")
    all_rows = group_rows * lax.axis_size("dp")
    scale = 2.0 / math.sqrt(group_rows * all_rows)
    return gradients(fingerprints, w_first, w_second, scale)


def solution(mesh):
    in_specs = (P(("blk", "dp"), None), P(), P())
    out_specs = (P("dp", None), P("dp", None))
    return jax.shard_map(
        per_device, mesh=mesh, in_specs=in_specs, out_specs=out_specs, check_vma=False
    )
```

```python
import functools
import math

import jax
import jax.numpy as jnp
from jax import lax
from jax.experimental import pallas as pl
from jax.experimental.pallas import tpu as pltpu
from jax.sharding import PartitionSpec as P

MESH = pl.DeviceIdType.MESH
F32 = jnp.float32
BF16 = jnp.bfloat16
NZ, NX = 8, 4
T = 256
PARTS = 2
SPLIT = (3, 2, 1)


def dot_nt(a, b):
    return lax.dot_general(a, b, (((1,), (1,)), ((), ())), preferred_element_type=F32)


def dot_nn(a, b):
    return jnp.dot(a, b, preferred_element_type=F32)


def step_kernel(
    scale, fp_in, w1_in, w2_in, o1, o2,
    fp, fpt, w1, w2, hid, hidt, emb, summed, gate, demb, dpre, sqc, sqr,
    gx, rx, gy, ry, gz, rz, hx, qx, hy, qy, hz, qz, kx, r3x, ky, qky, kz, r3z, f1, r1, f2, r2,
    ready, load_sem, send_sem, recv_sem, pass_send, pass_recv,
    xs, xr, ys, yr, zs, zr, xs2, xr2, ys2, yr2, zs2, zr2, xs3, xr3, s3, t3, zs3, zr3, s4, t4,
):
    blk = lax.axis_index("blk")
    dp = lax.axis_index("dp")
    z, x = dp // 8, (dp // 2) % 4
    y, c = (blk // 2) * 2 + dp % 2, blk % 2
    tok, d_in = fp_in.shape
    hidden, width = w2_in.shape
    half = 2 * tok
    rows_all = 4 * tok
    pieces = len(SPLIT)
    sizes = [tok * share // sum(SPLIT) for share in SPLIT]
    firsts = [sum(sizes[:p]) for p in range(pieces)]
    norm = 1.0 / math.sqrt(width)

    def at(z, x, y, c):
        return {"blk": (y // 2) * 2 + c, "dp": (z * NX + x) * 2 + y % 2}

    side = y % 2
    far = at(z, x, (y + 2) % 4, c)
    near = at(z, x, y, 1 - c)
    cross_far = at(z, x, (y + 2) % 4, 1 - c)
    pair = at(z, x, (y // 2) * 2 + 1 - side, c)
    x_peers = [at(z, (x + k) % NX, y, c) for k in range(1, NX)]
    z_peers = [at((z + k) % NZ, x, y, c) for k in range(1, NZ)]
    steps = [z_peers[k % NZ - 1] for k in (2, -2)]
    peers = [far, near, cross_far, pair] + x_peers + steps + [z_peers[0], z_peers[NZ - 2]]

    barrier = pltpu.get_barrier_semaphore()
    for peer in peers:
        pl.semaphore_signal(barrier, inc=1, device_id=peer, device_id_type=MESH)
    loads = [
        pltpu.make_async_copy(fp_in, fp.at[pl.ds(0, tok)], load_sem.at[0]),
        pltpu.make_async_copy(w1_in, w1, load_sem.at[1]),
        pltpu.make_async_copy(w2_in, w2, load_sem.at[2]),
    ]
    loads[0].start()
    pl.semaphore_wait(barrier, len(peers))

    def remote(src, dst, send, recv, peer):
        return pltpu.make_async_remote_copy(
            src_ref=src, dst_ref=dst, send_sem=send, recv_sem=recv,
            device_id=peer, device_id_type=MESH,
        )

    pending = []

    def landed(copy):
        copy.wait_recv()
        pending.append(copy)

    def far_copy(p):
        return remote(
            fp_in.at[pl.ds(firsts[p], sizes[p])],
            fp.at[pl.ds(half + 2 * firsts[p], sizes[p])],
            send_sem.at[p], recv_sem.at[p], far,
        )

    def passing(p):
        return remote(
            fp.at[pl.ds(half + 2 * firsts[p], sizes[p])],
            fp.at[pl.ds(half + 2 * firsts[p] + sizes[p], sizes[p])],
            pass_send.at[p], pass_recv.at[p], near,
        )

    near_copy = remote(
        fp_in, fp.at[pl.ds(tok, tok)], send_sem.at[pieces], recv_sem.at[pieces], near
    )
    for p in range(pieces):
        far_copy(p).start()
    near_copy.start()
    for load in loads[1:]:
        load.start()
    for peer in steps:
        pl.semaphore_signal(ready, inc=1, device_id=peer, device_id_type=MESH)
    for load in loads:
        load.wait()
    landed(near_copy)

    def encode_columns(rows, cols):
        pre = dot_nn(fp[rows, :], w1[:, cols])
        sig = 1.0 / (1.0 + jnp.exp(-pre))
        h = (pre * sig).astype(BF16)
        hid[pl.ds(0, h.shape[0]), cols] = h
        hidt[cols, rows] = h.T
        gate[rows, cols] = sig * (1.0 + pre * (1.0 - sig))

    def embed(rows, count):
        emb[rows, :] = dot_nn(hid[pl.ds(0, count), :], w2[...]).astype(BF16)

    def residual(upper, lower):
        inter = dot_nt(fp[upper, :], fp[lower, :])
        den = sqc[upper, :][:, :1] + sqr[:1, lower] - inter
        pred = dot_nt(emb[upper, :], emb[lower, :])
        return (pred * norm - inter / den).astype(BF16)

    def diagonal(first, count):
        rows = pl.ds(first, count)
        inter = dot_nt(fp[rows, :], fp[rows, :])
        r_id = lax.broadcasted_iota(jnp.int32, (count, count), 0)
        c_id = lax.broadcasted_iota(jnp.int32, (count, count), 1)
        diag = jnp.where(r_id == c_id, inter, 0.0)
        col = jnp.sum(diag, axis=1, keepdims=True)
        row = jnp.sum(diag, axis=0, keepdims=True)
        sqc[rows, :] = jnp.broadcast_to(col, (count, 128))
        sqr[:, rows] = jnp.broadcast_to(row, (8, count))
        pred = dot_nt(emb[rows, :], emb[rows, :])
        resid = (pred * norm - inter / (col + row - inter)).astype(BF16)
        summed[rows, :] = dot_nn(resid, emb[rows, :])

    def cross(upper, lower):
        resid = residual(upper, lower)
        summed[upper, :] += dot_nn(resid, emb[lower, :])
        summed[lower, :] += dot_nn(resid.T, emb[upper, :])

    @pl.loop(0, hidden // T)
    def _(n):
        cols = pl.ds(pl.multiple_of(n * T, T), T)
        encode_columns(pl.ds(0, half), cols)

    @pl.loop(0, d_in // T)
    def _(n):
        cols = pl.ds(pl.multiple_of(n * T, T), T)
        fpt[cols, pl.ds(0, half)] = fp[pl.ds(0, half), cols].T

    embed(pl.ds(0, half), half)
    pl.semaphore_wait(ready, len(steps))
    for r in range(0, half, T):
        diagonal(r, T)
        if r:
            cross(pl.ds(0, r), pl.ds(r, T))

    for p in range(pieces):
        first, count = half + 2 * firsts[p], 2 * sizes[p]
        rows = pl.ds(first, count)
        landed(far_copy(p))
        passing(p).start()
        landed(passing(p))
        for n in range(0, hidden, T):
            encode_columns(rows, pl.ds(n, T))
        for n in range(0, d_in, T):
            fpt[pl.ds(n, T), rows] = fp[rows, pl.ds(n, T)].T
        embed(rows, count)
        diagonal(first, count)
        cross(pl.ds(0, half), rows)
        if p:
            cross(pl.ds(half, first - half), rows)

    quarter = pl.ds(pl.multiple_of(blk * T, T), T)
    for r in range(0, rows_all, 2 * T):
        rows = pl.ds(r, 2 * T)
        part = (summed[rows, :] * scale).astype(BF16)
        demb[rows, :] = part
        back = dot_nt(part, w2[quarter, :])
        dpre[rows, :] = (back * gate[rows, quarter]).astype(BF16)

    x_copies, y_copies = [], []
    span = NZ // PARTS
    own = gy.shape[3]
    for i in range(PARTS):
        rows = pl.ds(i * d_in // PARTS, d_in // PARTS)
        part = dot_nn(fpt[rows, :], dpre[...]).astype(BF16)
        for k in range(span):
            zz = i * span + k
            for xx in range(NX):
                for ll in range(2):
                    line = ((k * NX + xx) * 2 + ll) * own
                    gx[xx, zz, ll * own : (ll + 1) * own, :] = part[line : line + own, :128]
                    gy[ll, zz, xx] = part[line : line + own, 128:]
        zz = pl.ds(i * span, span)
        copy = remote(gy.at[1 - side, zz], ry.at[zz], ys.at[i], yr.at[i], pair)
        y_copies.append(copy)
        copy.start()
        for k in (2, 1, 3):
            copy = remote(
                gx.at[(x + k) % NX, zz], rx.at[k - 1, zz],
                xs.at[i, k - 1], xr.at[i, k - 1], x_peers[k - 1],
            )
            x_copies.append(copy)
            copy.start()

    cols = width // 4
    part = dot_nn(hidt[...], demb[:, pl.ds(pl.multiple_of(blk * cols, cols), cols)])
    gz[...] = part.astype(BF16).reshape(gz.shape)
    z_copies = [
        remote(gz.at[(z + k) % NZ], rz.at[k - 1], zs.at[k - 1], zr.at[k - 1], z_peers[k - 1])
        for k in (4, 3, 5, 2, 6, 1, 7)
    ]
    for copy in z_copies:
        copy.start()

    def total(mine, others):
        out = mine.astype(F32)
        for k in range(others.shape[0]):
            out = out + others[k].astype(F32)
        return out

    more = []
    for i in range(PARTS):
        landed(y_copies[i])
        zz = pl.ds(i * span, span)
        for xx in range(NX):
            hy[xx, zz] = (gy[side, zz, xx].astype(F32) + ry[zz, xx].astype(F32)).astype(BF16)
        for k in (2, 1, 3):
            copy = remote(
                hy.at[(x + k) % NX, zz], qy.at[k - 1, zz],
                ys2.at[i, k - 1], yr2.at[i, k - 1], x_peers[k - 1],
            )
            more.append(copy)
            copy.start()
    y_copies = more

    for copy in x_copies:
        landed(copy)
    hx[...] = total(gx[x], rx).astype(BF16)
    x_copies = [
        remote(hx.at[(z + k) % NZ], qx.at[k - 1], xs2.at[k - 1], xr2.at[k - 1], z_peers[k - 1])
        for k in (4, 3, 5, 2, 6, 1, 7)
    ]
    for copy in x_copies:
        copy.start()

    def level(zz):
        return remote(
            ky.at[zz], qky.at[z], s3.at[zz], t3.at[z], at(zz, x, y, c)
        )

    def arrival(zz):
        return remote(
            ky.at[zz], qky.at[zz], s3.at[zz], t3.at[zz], at(zz, x, y, c)
        )

    for i in range(PARTS):
        for copy in y_copies[i * (NX - 1) : (i + 1) * (NX - 1)]:
            landed(copy)
        for zz in range(i * span, (i + 1) * span):
            ky[zz] = total(hy[x, zz], qy[:, zz])

            @pl.when(z != zz)
            def _(zz=zz):
                level(zz).start()

    for copy in z_copies:
        landed(copy)
    hz[...] = total(gz[z], rz).reshape(hz.shape)
    z_copies = [
        remote(hz.at[(x + k) % NX], qz.at[k - 1], zs2.at[k - 1], zr2.at[k - 1], x_peers[k - 1])
        for k in (2, 1, 3)
    ]
    for copy in z_copies:
        copy.start()

    for copy in z_copies:
        landed(copy)
    kz[...] = total(hz[x], qz).reshape(kz.shape)
    z_copy = remote(kz.at[1 - side], r3z, zs3, zr3, pair)
    z_copy.start()
    for copy in x_copies:
        landed(copy)
    kx[...] = total(hx[z], qx).reshape(kx.shape)
    x_copy = remote(kx.at[1 - side], r3x, xs3, xr3, pair)
    x_copy.start()
    landed(z_copy)
    f2[...] = kz[side] + r3z[...]

    def spread(src, dst, i):
        out = [
            remote(src, dst.at[blk], s4.at[i, k], t4.at[i, k], peer)
            for k, peer in enumerate((cross_far, far, near))
        ]
        for copy in out:
            copy.start()
        return out

    last = spread(f2, r2, 0)
    landed(x_copy)
    f1[0] = kx[side] + r3x[...]
    last += spread(f1.at[0], r1.at[0], 1)
    qky[z] = ky[z]
    for zz in range(NZ):

        @pl.when(z != zz)
        def _(zz=zz):
            arrival(zz).wait()

    part = qky[0]
    for zz in range(1, NZ):
        part = part + qky[zz]
    f1[1] = part
    last += spread(f1.at[1], r1.at[1], 2)
    for i in range(2):
        r1[i, blk] = f1[i]
    r2[blk] = f2[...]
    for copy in last:
        landed(copy)
    for copy in pending:
        copy.wait_send()
    for q in range(4):
        for i in range(2):
            o1[:, (2 * q + i) * 128 : (2 * q + i + 1) * 128] = r1[i, q]
        o2[:, q * o2.shape[1] // 4 : (q + 1) * o2.shape[1] // 4] = r2[q]


def gradients(fingerprints, w_first, w_second, scale):
    tok, d_in = fingerprints.shape
    hidden, width = w_second.shape
    rows = 4 * tok
    pieces = len(SPLIT)
    hbm_spec = pl.BlockSpec(memory_space=pltpu.HBM)
    vmem_spec = pl.BlockSpec(memory_space=pltpu.VMEM)
    c1, c2 = hidden // 4, width // 4
    n1, n2 = d_in // (NZ * NX * 2), hidden // (NZ * NX * 2)
    dma = pltpu.SemaphoreType.DMA
    return pl.pallas_call(
        functools.partial(step_kernel, scale),
        out_shape=(
            jax.ShapeDtypeStruct((n1, 4 * c1), F32),
            jax.ShapeDtypeStruct((n2, 4 * c2), F32),
        ),
        in_specs=[hbm_spec] * 3,
        out_specs=(vmem_spec, vmem_spec),
        scratch_shapes=[
            pltpu.VMEM((rows, d_in), BF16),
            pltpu.VMEM((d_in, rows), BF16),
            pltpu.VMEM((d_in, hidden), BF16),
            pltpu.VMEM((hidden, width), BF16),
            pltpu.VMEM((2 * tok, hidden), BF16),
            pltpu.VMEM((hidden, rows), BF16),
            pltpu.VMEM((rows, width), BF16),
            pltpu.VMEM((rows, width), F32),
            pltpu.VMEM((rows, hidden), F32),
            pltpu.VMEM((rows, width), BF16),
            pltpu.VMEM((rows, hidden // 4), BF16),
            pltpu.VMEM((rows, 128), F32),
            pltpu.VMEM((8, rows), F32),
            pltpu.VMEM((NX, NZ, 2 * n1, 128), BF16),
            pltpu.VMEM((NX - 1, NZ, 2 * n1, 128), BF16),
            pltpu.VMEM((2, NZ, NX, n1, 128), BF16),
            pltpu.VMEM((NZ, NX, n1, 128), BF16),
            pltpu.VMEM((NZ, NX * 2 * n2, c2), BF16),
            pltpu.VMEM((NZ - 1, NX * 2 * n2, c2), BF16),
            pltpu.VMEM((NZ, 2 * n1, 128), BF16),
            pltpu.VMEM((NZ - 1, 2 * n1, 128), BF16),
            pltpu.VMEM((NX, NZ, n1, 128), BF16),
            pltpu.VMEM((NX - 1, NZ, n1, 128), BF16),
            pltpu.VMEM((NX, 2 * n2, c2), F32),
            pltpu.VMEM((NX - 1, 2 * n2, c2), F32),
            pltpu.VMEM((2, n1, 128), F32),
            pltpu.VMEM((n1, 128), F32),
            pltpu.VMEM((NZ, n1, 128), F32),
            pltpu.VMEM((NZ, n1, 128), F32),
            pltpu.VMEM((2, n2, c2), F32),
            pltpu.VMEM((n2, c2), F32),
            pltpu.VMEM((2, n1, 128), F32),
            pltpu.VMEM((2, 4, n1, 128), F32),
            pltpu.VMEM((n2, c2), F32),
            pltpu.VMEM((4, n2, c2), F32),
            pltpu.SemaphoreType.REGULAR,
            dma((3,)),
            dma((pieces + 1,)),
            dma((pieces + 1,)),
            dma((pieces,)),
            dma((pieces,)),
            dma((PARTS, NX - 1)),
            dma((PARTS, NX - 1)),
            dma((PARTS,)),
            dma((PARTS,)),
            dma((NZ - 1,)),
            dma((NZ - 1,)),
            dma((NZ - 1,)),
            dma((NZ - 1,)),
            dma((PARTS, NX - 1)),
            dma((PARTS, NX - 1)),
            dma((NX - 1,)),
            dma((NX - 1,)),
            dma,
            dma,
            dma((NZ,)),
            dma((NZ,)),
            dma,
            dma,
            dma((3, 3)),
            dma((3, 3)),
        ],
        compiler_params=pltpu.CompilerParams(
            collective_id=0, has_side_effects=True, vmem_limit_bytes=55500000
        ),
        name="gradients",
    )(fingerprints, w_first, w_second)


def per_device(fingerprints, w_first, w_second):
    group_rows = fingerprints.shape[0] * lax.axis_size("blk")
    all_rows = group_rows * lax.axis_size("dp")
    scale = 2.0 / math.sqrt(group_rows * all_rows)
    return gradients(fingerprints, w_first, w_second, scale)


def solution(mesh):
    in_specs = (P(("blk", "dp"), None), P(), P())
    out_specs = (P("dp", None), P("dp", None))
    return jax.shard_map(
        per_device, mesh=mesh, in_specs=in_specs, out_specs=out_specs, check_vma=False
    )
```
